32 devices in a mesh: row: 8 (over z, x), col: 4 (over y, core).
Axes of the slice: x: 2, y: 2, z: 4, core: 2. Of those that a mesh axis runs over, the one named last changes fastest.
Arguments:
- subspace: bfloat16 [256, 32768], P('col', 'row'), may hold values from -400 to 400
- onsite: float32 [32768], P('row'), may hold values from -1.5 to 1.5
- blocks: bfloat16 [20, 256, 128, 128], P(None, 'row'), may hold values from -0.125 to 0.125
- cols: int32 [256, 20], replicated, may hold values from 0 to 255, as said below
Outputs:
- basis: float32 [256, 32768], P('col', 'row')
- factor: float32 [256, 256], replicated
The draws below stay inside these ranges and needn't reach their ends.
Inputs may be any that keep to these rules, and one draw needn't show every extreme that they name: `cols`: the block rows are numbered by device: device r of row holds block rows r * 32 to (r + 1) * 32 - 1. A block row names block rows of its own device or of the devices r + 1, r - 1, r + 2 and r + 4 along row, counted round. The block rows of one device name between 1 and 4 distinct block rows of each of these four devices, and in every draw some device names exactly 4 on each of its four.
All inputs are finite; a program needn't handle non-finite values.
Results may differ from the reference program's by a relative error of at most 0.0044.
Values may be sent and summed in bfloat16 or wider, within the bound.
A program may use at most 128 MiB of HBM per device.

```python
import math
import jax
import jax.numpy as jnp
from jax import lax

BS = 128
NNZ = 20
S = 256
HALO = 4
FILTER = 4
BR_DEV = 32
NB = 256
NTOT = 32768


remote_slots = 4


def draw_cols(key, part):
    row_count = NB // BR_DEV
    keys = jax.random.split(jax.random.fold_in(key, 7), 5)
    counts = jax.random.randint(keys[0], (row_count, 4), 1, HALO + 1)
    busiest = jax.random.randint(keys[1], (), 0, row_count)
    counts = jnp.where(jnp.arange(row_count)[:, None] == busiest, HALO, counts)
    scores = jax.random.randint(keys[2], (row_count, 4, BR_DEV), 0, 2 ** 20) * BR_DEV + jnp.arange(BR_DEV)
    orders = jnp.argsort(scores, axis=-1).astype(jnp.int32)
    local_rows = jnp.arange(BR_DEV)[:, None]
    slot_ids = jnp.arange(NNZ)[None, :]
    pair_ids = (local_rows * remote_slots + slot_ids) % (4 * HALO)
    group_ids = pair_ids // HALO
    member_ids = pair_ids % HALO
    device_ids = jnp.arange(row_count)[:, None, None]
    valid = (slot_ids < remote_slots)[None] & (member_ids[None] < counts[device_ids, group_ids[None]])
    offsets = jnp.array([1, -1, 2, row_count // 2], dtype=jnp.int32)
    owners = (device_ids + offsets[group_ids][None]) % row_count
    chosen = orders[device_ids, group_ids[None], member_ids[None]]
    remote = owners * BR_DEV + chosen
    local = jax.random.randint(keys[3], (row_count, BR_DEV, NNZ), 0, BR_DEV) + device_ids * BR_DEV
    named = jnp.where(valid, remote, local)
    slot_scores = jax.random.randint(keys[4], (row_count, BR_DEV, NNZ), 0, 2 ** 20) * NNZ + jnp.arange(NNZ)
    slot_order = jnp.argsort(slot_scores, axis=-1)
    named = jnp.take_along_axis(named, slot_order, axis=-1)
    return named.reshape(NB, NNZ).astype(jnp.int32)


def draw_subspace(key, part):
    keys = jax.random.split(jax.random.fold_in(key, 11), 3)
    values = jax.random.normal(keys[0], (S, NTOT), jnp.float32)
    column_scale = jnp.exp(jax.random.uniform(keys[1], (S, 1), jnp.float32) * math.log(10.0))
    row_scale = jnp.exp(jax.random.uniform(keys[2], (1, NTOT), jnp.float32) * math.log(10.0))
    row_scale = row_scale * 3.0 ** (jnp.arange(NTOT, dtype=jnp.float32)[None, :] / NTOT)
    return (0.1 * values * column_scale * row_scale).astype(jnp.bfloat16)


def level_of(stream_key, dims, cuts, smallest, largest):
    def one(axis_at, blocks):
        draws = jax.random.uniform(jax.random.fold_in(jax.random.fold_in(stream_key, 6), axis_at), (blocks,), jnp.float32, smallest / len(cuts), largest / len(cuts))
        return jnp.repeat(jnp.exp(draws), dims[axis_at] // blocks).reshape((-1,) + (1,) * (len(dims) - axis_at - 1))

    loudness = one(*cuts[0])
    for cut in cuts[1:]:
        loudness = loudness * one(*cut)
    return loudness


def noise(key, extent, deviation, bound, cuts=(), kind=jnp.bfloat16):
    level = level_of(key, extent, cuts, -0.22, 0.18) if cuts else 1.0
    entries = jax.random.normal(key, extent, jnp.float32) * deviation * level
    return jnp.minimum(jnp.maximum(entries, -bound), bound).astype(kind)


def setup_inputs(seed: int = 0) -> dict:
    key_list = jax.random.split(jax.random.key(seed), 5)
    subspace = draw_subspace(jax.random.fold_in(key_list[4], 71), 0)
    onsite = jnp.clip(jax.random.uniform(key_list[1], (NTOT,), jnp.float32, -1.5, 1.5) * level_of(key_list[1], (NTOT,), ((0, 8),), -0.4, 0.0), -1.5, 1.5)
    blocks = noise(key_list[2], (NNZ, NB, BS, BS), (NNZ * BS) ** -0.5, 0.125, ((1, 8),))
    cols = draw_cols(jax.random.fold_in(key_list[4], 71), 0)
    return {"subspace": subspace, "onsite": onsite, "blocks": blocks, "cols": cols}


filter_scale = 0.4

def couple(lowered, onsite, blocks, cols):
    shaped = lowered.reshape(S, NB, BS)

    def add_slot(total, pair):
        slot_cols, slot_blocks = pair
        taken = jnp.take(shaped, slot_cols, axis=1).astype(jnp.float32)
        return (total + jnp.einsum('cla,lab->clb', taken, slot_blocks.astype(jnp.float32)), None)
    total, _ = lax.scan(add_slot, jnp.zeros((S, NB, BS), jnp.float32), (cols.T, blocks))
    return total.reshape(S, NTOT) + onsite[None, :] * lowered.astype(jnp.float32)

def reference(subspace, onsite, blocks, cols):
    previous = subspace.astype(jnp.float32)
    current = filter_scale * couple(subspace, onsite, blocks, cols)
    for filter_step in range(FILTER - 1):
        lowered = current.astype(jnp.bfloat16)
        following = 2.0 * filter_scale * couple(lowered, onsite, blocks, cols) - previous
        previous, current = (current, following)
    final = current.astype(jnp.bfloat16)
    gram = jnp.dot(final.astype(jnp.float32), final.T.astype(jnp.float32), preferred_element_type=jnp.float32)
    lower = jnp.linalg.cholesky(gram)
    inverse = lax.linalg.triangular_solve(lower, jnp.eye(S, dtype=jnp.float32), left_side=True, lower=True)
    basis = math.sqrt(NTOT) * jnp.dot(inverse, final.astype(jnp.float32), precision=lax.Precision.HIGHEST)
    factor = lower.T / math.sqrt(NTOT)
    return (basis, factor)
```

```python
import functools
import math

import jax
import jax.numpy as jnp
from jax import lax
from jax.experimental import pallas as pl
from jax.experimental.pallas import tpu as pltpu
from jax.sharding import PartitionSpec as P

HALO = 4
FILTER = 4
UNROLL = 4
HALVES = 1
filter_scale = 0.4
f32 = jnp.float32
bf16 = jnp.bfloat16


def shifts_of(rows):
    return (rows // 2, 2, 1, -1)


def index_tables(cols, rows, me, lb):
    sc = cols.shape[1]
    shifts = shifts_of(rows)
    groups = len(shifts)
    own = lax.dynamic_slice_in_dim(cols, me * lb, lb, 0).reshape(-1)
    askers = [
        lax.dynamic_slice_in_dim(cols, lax.rem(me - d + rows, rows) * lb, lb, 0).reshape(-1)
        for d in shifts
    ]
    owners = jnp.stack([lax.rem(me + d + rows, rows) for d in shifts])
    k = jnp.arange(lb, dtype=jnp.int32)
    wanted = own[None, :] - owners[:, None] * lb
    asked = jnp.stack(askers) - me * lb
    rel = jnp.concatenate([wanted, asked], 0)
    hit = jnp.any(rel[:, :, None] == k, axis=1)
    before = (k[:, None] < k[None, :])
    rank = jnp.sum((hit[:, :, None] & before[None]).astype(jnp.int32), axis=1)
    hit_e, rank_e = hit[groups:], rank[groups:]
    g = jnp.arange(groups, dtype=jnp.int32)
    key = jnp.min(jnp.where(hit_e, g[:, None], groups), axis=0)
    ahead = (key[:, None] < key[None, :]) | ((key[:, None] == key[None, :]) & before)
    inv = jnp.sum(ahead.astype(jnp.int32), axis=0)
    perm = jnp.sum(jnp.where(inv[None, :] == k[:, None], k[None, :], 0), axis=1)
    m = jnp.arange(HALO, dtype=jnp.int32)
    pick = hit_e[:, None, :] & (rank_e[:, None, :] == m[:, None])
    exp_n = jnp.sum(jnp.where(pick, k, 0), axis=-1)
    exp_p = jnp.sum(jnp.where(pick, inv, 0), axis=-1)
    slot = lb + HALO * g[:, None] + rank[:groups]
    match = wanted[:, :, None] == k
    far = jnp.sum(jnp.where(match, slot[:, None, :], 0), axis=(0, 2))
    near = own - me * lb
    mine = (near >= 0) & (near < lb)
    near_p = jnp.sum(jnp.where(near[:, None] == k, inv, 0), axis=1)
    pos_n = jnp.where(mine, near, far)
    pos_p = jnp.where(mine, near_p, far)
    return jnp.concatenate(
        [pos_n, pos_p, perm, inv, exp_n.reshape(-1), exp_p.reshape(-1)]
    ).astype(jnp.int32)


def flip(c, bit):
    return c + bit - 2 * bit * lax.rem(c // bit, 2)


def hops_of(parts):
    hops, held, bit = [], [0], parts // 2
    while bit:
        hops += [(bit, m) for m in held]
        held += [m + bit for m in held]
        bit //= 2
    return hops


def slice_of(width, rows):
    return max(8, width // rows)


def filter_kernel(rows, parts, lb, sc, tab, sub, ons, blk, out, gram, bm, *refs):
    refs = list(refs)
    take = lambda n: [refs.pop(0) for _ in range(n)]
    halves = range(HALVES)
    xs = [take(HALVES) for _ in range(FILTER)]
    snds = [take(HALVES) for _ in range(FILTER)]
    ys = [take(HALVES) for _ in range(FILTER - 1)]
    s0 = take(HALVES)
    gp, gs, rb, bsem, xsem, csem, ssem, rsem, wss, wrs, pss, prs, ass, ars = refs
    me = lax.axis_index("row")
    mc = lax.axis_index("col")
    everyone = rows * parts
    linear = me * parts + mc
    hw = out.shape[2]
    width = hw * HALVES
    hops = hops_of(parts)
    rps = slice_of(width, rows)
    reducers = width // rps
    shifts = shifts_of(rows)
    groups = len(shifts)
    pn, pp = 0, lb * sc
    pperm = 2 * lb * sc
    pinv = pperm + lb
    pexn = pinv + lb
    pexp = pexn + groups * HALO
    bs = blk.shape[-1]
    chunks = lb // UNROLL

    def load(c):
        part = pl.ds(c * UNROLL, UNROLL)
        return pltpu.make_async_copy(blk.at[:, part], bm.at[:, part], bsem.at[c])

    def first(i, h):
        cut = sub.at[pl.ds(h * hw, hw), pl.ds(pl.multiple_of(i * bs, bs), bs)]
        return (pltpu.make_async_copy(cut, xs[0][h].at[i], xsem.at[h, i]),
                pltpu.make_async_copy(cut, s0[h].at[i], csem.at[h, i]))

    for h in halves:
        @pl.loop(0, lb)
        def _(i):
            a, b = first(i, h)
            b.start()
            a.start()

    @pl.loop(0, chunks)
    def _(c):
        load(c).start()

    barrier = pltpu.get_barrier_semaphore()

    @pl.loop(1, everyone)
    def _(e):
        to = lax.rem(linear + e, everyone)
        pl.semaphore_signal(barrier, inc=1, device_id=(to // parts, lax.rem(to, parts)),
                            device_id_type=pl.DeviceIdType.MESH)

    def copy(k, h, g):
        return pltpu.make_async_remote_copy(
            src_ref=snds[k][h].at[pl.ds(g * HALO, HALO)],
            dst_ref=xs[k][h].at[pl.ds(lb + g * HALO, HALO)],
            send_sem=ssem.at[k, h, g], recv_sem=rsem.at[k, h, g],
            device_id=(lax.rem(me - shifts[g] + rows, rows), mc),
            device_id_type=pl.DeviceIdType.MESH)

    def pack(k, h, g, source, base):
        for m in range(HALO):
            snds[k][h][g * HALO + m] = source[tab[base + g * HALO + m]].astype(bf16)

    for h in halves:
        @pl.loop(0, lb)
        def _(i):
            first(i, h)[1].wait()

        for g in range(groups):
            pack(0, h, g, s0[h], pexn)
        if h == 0:
            pl.semaphore_wait(barrier, everyone - 1)
        for g in range(groups):
            copy(0, h, g).start()

    for h in halves:
        @pl.loop(0, lb)
        def _(i):
            first(i, h)[0].wait()

    def place(k, j):
        i = j if k == FILTER - 1 else tab[pperm + j]
        own = tab[pinv + j] if k == FILTER - 1 else (i if k == 0 else j)
        return i, own

    def feed(k, first_row, accs):
        base = pn if k == 0 else pp
        x = xs[k][0]
        at = [place(k, first_row + u)[0] for u in range(UNROLL)]
        for t in range(sc // 2):
            for m in range(2):
                pair = at[2 * m:2 * m + 2]
                pltpu.matmul_push_rhs(jnp.concatenate(
                    [jnp.concatenate([bm[2 * t, i], bm[2 * t + 1, i]], axis=0) for i in pair],
                    axis=1), t % 2, m)
                for u, i in enumerate(pair):
                    left = jnp.concatenate(
                        [x[tab[base + i * sc + 2 * t + s]] for s in range(2)], axis=1)
                    pltpu.matmul_acc_lhs(accs[m][u], left,
                                         load_staged_rhs=t % 2 if u == 0 else None)

    def settle(k, row, acc, u):
        i, own = place(k, row)
        total = pltpu.matmul_pop(acc)[:, u * bs:(u + 1) * bs]
        total = total + ons[i] * xs[k][0][own].astype(f32)
        if k == 0:
            return filter_scale * total
        prev = xs[0][0][i].astype(f32) if k == 1 else ys[k - 2][0][own]
        return 2.0 * filter_scale * total - prev

    def turn(piece, c):
        return lax.rem(c + (1 - piece // (parts // 2)) * (chunks // 2), chunks)

    def spread(n, h, c):
        bit, m = hops[n]
        piece = mc
        for b in (m & (1 << t) for t in range(m.bit_length())):
            if b:
                piece = flip(piece, b)
        part = out.at[piece * HALVES + h, pl.ds(turn(piece, c) * UNROLL, UNROLL)]
        return pltpu.make_async_remote_copy(
            src_ref=part, dst_ref=part, send_sem=wss.at[n, h, c], recv_sem=wrs.at[n, h, c],
            device_id=(me, flip(mc, bit)), device_id_type=pl.DeviceIdType.MESH)

    firsts = [n for n, (_, m) in enumerate(hops) if m == 0]

    @pl.loop(0, chunks)
    def _(c):
        load(c).wait()

    def keep(k, j, value):
        low = value.astype(bf16)
        if k < FILTER - 1:
            xs[k + 1][0][j] = low
            ys[k][0][j] = value
        else:
            out[mc, j] = low

    def rows_of(k, c):
        return (turn(mc, c) if k == FILTER - 1 else c) * UNROLL

    def chunk(k, c, accs):
        for m in range(2):
            for u in range(2):
                j = rows_of(k, c) + 2 * m + u
                keep(k, j, settle(k, j, accs[m][u], u))

    def filtering(*flat):
        sets = [[flat[4 * q + 2 * m:4 * q + 2 * m + 2] for m in range(2)] for q in range(2)]
        for k in range(FILTER):
            for g in range(groups):
                copy(k, 0, g).wait_recv()
            ahead = groups if k < FILTER - 1 else 0
            for c in range(0, ahead, 2):
                for q in range(2):
                    feed(k, rows_of(k, c + q), sets[q])
                if c:
                    copy(k + 1, 0, c - 1).start()
                for q in range(2):
                    chunk(k, c + q, sets[q])
                    if q:
                        copy(k + 1, 0, c).start()
                    pack(k + 1, 0, c + q, ys[k][0], pexp)

            @pl.loop(ahead // 2, chunks // 2)
            def _(cc):
                for q in range(2):
                    feed(k, rows_of(k, 2 * cc + q), sets[q])
                if ahead:
                    @pl.when(cc == ahead // 2)
                    def _():
                        copy(k + 1, 0, ahead - 1).start()
                for q in range(2):
                    chunk(k, 2 * cc + q, sets[q])
                if k == FILTER - 1:
                    @pl.when(cc > 0)
                    def _():
                        for n in firsts:
                            for q in range(2):
                                spread(n, 0, 2 * cc - 2 + q).start()
            if k == FILTER - 1:
                for n in firsts:
                    for q in range(2):
                        spread(n, 0, chunks - 2 + q).start()

    pl.run_scoped(filtering, *[pltpu.ACC(m)((width, 2 * bs), f32)
                               for _ in range(2) for m in range(2) for _ in range(2)])

    for k in range(FILTER):
        for h in halves:
            for g in range(groups):
                copy(k, h, g).wait_send()

    needs = {n: max(q for q in range(n) if sum(hops[q]) == m)
             for n, (_, m) in enumerate(hops) if m}
    def relay(lo, hi):
        for h in halves:
            @pl.loop(lo, hi)
            def _(c):
                got = set()
                for n in needs:
                    if needs[n] not in got:
                        spread(needs[n], h, c).wait_recv()
                        got.add(needs[n])
                    spread(n, h, c).start()

    def arrive(lo, hi, picked):
        for h in halves:
            @pl.loop(lo, hi)
            def _(c):
                for n in picked:
                    spread(n, h, c).wait_recv()

    top = parts // 2
    leaves = [n for n in range(len(hops)) if n not in needs.values()]
    near = [n for n in leaves if sum(hops[n]) < top]
    other = [n for n in leaves if sum(hops[n]) >= top]
    relay(0, chunks // 2)
    arrive(0, chunks, near)
    arrive(0, chunks // 2, other)

    side = mc // top
    half = lb // 2

    def tall(q, first_row):
        return jnp.concatenate([out[q, first_row], out[q, first_row + 1]], axis=1)

    def gramming(*accs):
        both, one, two = [accs[2 * n:2 * n + 2] for n in range(3)]

        @pl.loop(0, half // 4)
        def _(c):
            for m in range(2):
                row = side * half + c * 4 + 2 * m
                pltpu.matmul_push_rhs(
                    jnp.concatenate([tall(q, row) for q in range(parts)], axis=0),
                    0, m, transpose=True)
                pltpu.matmul_acc_lhs(both[m], tall(mc, row), load_staged_rhs=0)

        @pl.loop(0, half // 8)
        def _(c):
            for m in range(2):
                row = (1 - side) * half + c * 8 + 4 * m
                pltpu.matmul_push_rhs(
                    jnp.concatenate([tall(side * top + q, row + r)
                                     for r in (0, 2) for q in range(top)], axis=0),
                    0, m, transpose=True)
                pltpu.matmul_acc_lhs(one[m], tall(mc, row), load_staged_rhs=0)
                pltpu.matmul_acc_lhs(two[m], tall(mc, row + 2))

        across = top * width
        gp[...] = pltpu.matmul_pop(both[0]) + pltpu.matmul_pop(both[1])
        cut = pl.ds(pl.multiple_of(side * across, across), across)
        near_sum = [pltpu.matmul_pop(one[m])[:, :across] + pltpu.matmul_pop(two[m])[:, across:]
                    for m in range(2)]
        gp[:, cut] += near_sum[0] + near_sum[1]

    pl.run_scoped(gramming, *[pltpu.ACC(m)((width, parts * width), f32)
                              for _ in range(3) for m in range(2)])

    def part_to(d):
        to = lax.rem(me + d, rows)
        lo = pl.multiple_of(to * rps, rps)
        return to, pltpu.make_async_remote_copy(
            src_ref=gp.at[pl.ds(lo, rps)], dst_ref=rb.at[d], send_sem=pss.at[d],
            recv_sem=prs.at[d], device_id=(to, mc), device_id_type=pl.DeviceIdType.MESH)

    def part_in(d):
        return pltpu.make_async_remote_copy(
            src_ref=gp.at[pl.ds(0, rps)], dst_ref=rb.at[d], send_sem=pss.at[d],
            recv_sem=prs.at[d], device_id=(lax.rem(me + 1, rows), mc),
            device_id_type=pl.DeviceIdType.MESH)

    def only(cond, run):
        if reducers == rows:
            run()
        else:
            pl.when(cond)(run)

    @pl.loop(1, rows)
    def _(d):
        to, c = part_to(d)
        only(to < reducers, lambda: c.start())

    def all_to(e, sender):
        to = lax.rem(linear + e, everyone)
        lo = pl.multiple_of((lax.rem(sender, parts) * reducers + sender // parts) * rps, rps)
        return pltpu.make_async_remote_copy(
            src_ref=gs, dst_ref=gram.at[pl.ds(lo, rps)], send_sem=ass.at[e],
            recv_sem=ars.at[e], device_id=(to // parts, lax.rem(to, parts)),
            device_id_type=pl.DeviceIdType.MESH)

    def reduce():
        lo = pl.multiple_of(me * rps, rps)
        total = gp[pl.ds(lo, rps)]
        for d in range(1, rows):
            part_in(d).wait_recv()
            total = total + rb[d]
        gs[...] = total
        gram[pl.ds(pl.multiple_of((mc * reducers + me) * rps, rps), rps)] = total

        @pl.loop(1, everyone)
        def _(e):
            all_to(e, linear).start()

    only(me < reducers, reduce)
    relay(chunks // 2, chunks)
    arrive(chunks // 2, chunks, other)
    for h in halves:
        @pl.loop(0, chunks)
        def _(c):
            for n in range(len(hops)):
                spread(n, h, c).wait_send()

    @pl.loop(1, rows)
    def _(d):
        to, c = part_to(d)
        only(to < reducers, lambda: c.wait_send())

    @pl.loop(1, everyone)
    def _(e):
        sender = lax.rem(linear - e + everyone, everyone)
        only(me < reducers, lambda: all_to(e, linear).wait_send())
        only(sender // parts < reducers, lambda: all_to(e, sender).wait_recv())


def filtered(subspace, onsite, blocks, cols):
    rows, parts = lax.axis_size("row"), lax.axis_size("col")
    me = lax.axis_index("row")
    everyone, hops = rows * parts, len(hops_of(parts))
    width = subspace.shape[0]
    sc, lb, bs, _ = blocks.shape
    groups = len(shifts_of(rows))
    tab = index_tables(cols, rows, me, lb)
    ext = lb + groups * HALO
    vm, dma = pltpu.VMEM, pltpu.SemaphoreType.DMA
    full, hw = parts * width, width // HALVES
    rps = slice_of(width, rows)
    return pl.pallas_call(
        functools.partial(filter_kernel, rows, parts, lb, sc),
        out_shape=(jax.ShapeDtypeStruct((parts * HALVES, lb, hw, bs), bf16),
                   jax.ShapeDtypeStruct((full, full), f32)),
        in_specs=[pl.BlockSpec(memory_space=pltpu.SMEM), pl.BlockSpec(memory_space=pl.ANY),
                  pl.BlockSpec(memory_space=pltpu.VMEM), pl.BlockSpec(memory_space=pl.ANY)],
        out_specs=[pl.BlockSpec(memory_space=pltpu.VMEM)] * 2,
        scratch_shapes=[vm((sc, lb, bs, bs), bf16)]
        + [vm((ext, hw, bs), bf16)] * (FILTER * HALVES)
        + [vm((groups * HALO, hw, bs), bf16)] * (FILTER * HALVES)
        + [vm((lb, hw, bs), f32)] * ((FILTER - 1) * HALVES)
        + [vm((lb, hw, bs), bf16)] * HALVES
        + [vm((width, full), f32), vm((rps, full), f32), vm((rows, rps, full), f32)]
        + [dma((lb // UNROLL,)), dma((HALVES, lb)), dma((HALVES, lb)),
           dma((FILTER, HALVES, groups)), dma((FILTER, HALVES, groups)),
           dma((hops, HALVES, lb // UNROLL)), dma((hops, HALVES, lb // UNROLL)),
           dma((rows,)), dma((rows,)), dma((everyone,)), dma((everyone,))],
        compiler_params=pltpu.CompilerParams(
            collective_id=0, has_side_effects=True, vmem_limit_bytes=56 * 1024 * 1024),
        name="filter",
    )(tab, subspace, onsite.reshape(lb, 1, bs), blocks)


def eliminate(src, up, low):
    n = src.shape[0]
    tiles = n // 8
    a = [src[8 * t:8 * t + 8, :] for t in range(tiles)]
    sub = lax.broadcasted_iota(jnp.int32, (8, n), 0)
    lane = lax.broadcasted_iota(jnp.int32, (8, n), 1)
    b = [jnp.where(lane == sub + 8 * t, 1.0, 0.0).astype(f32) for t in range(tiles)]

    def row(v, q):
        return jnp.broadcast_to(v[q:q + 1, :], (8, n))

    for p in range(tiles):
        cols = {t: [jnp.broadcast_to(a[t][:, 8 * p + q:8 * p + q + 1], (8, n)) for q in range(8)]
                for t in range(p, tiles)}
        pivots = jnp.ones((8, n), f32)
        for q in range(8):
            pivot = row(cols[p][q], q)
            pivots = jnp.where(sub == q, pivot, pivots)
            inverse = 1.0 / pivot
            right = [row(cols[p][k], q) for k in range(8)]
            arow, brow = row(a[p], q), row(b[p], q)
            for t in range(p, tiles):
                m = cols[t][q] * inverse
                if t == p:
                    m = jnp.where(sub > q, m, 0.0)
                for k in range(q + 1, 8):
                    cols[t][k] = cols[t][k] - m * right[k]
                a[t] = a[t] - m * arow
                b[t] = b[t] - m * brow
        scale = lax.rsqrt(pivots)
        up[8 * p:8 * p + 8, :] = jnp.where(lane >= sub + 8 * p, a[p] * scale, 0.0)
        low[8 * p:8 * p + 8, :] = b[p] * scale


def finish_kernel(root, col, stored, gram, basis, factor, work, up, low, inv, whole, sem):
    fetch = pltpu.make_async_copy(stored, whole, sem)
    fetch.start()
    parts, lb, _, bs = whole.shape
    width = basis.shape[0]
    full = gram.shape[0]
    half = full // 2
    exact = functools.partial(lax.dot_general, precision=lax.Precision.HIGHEST,
                              preferred_element_type=f32)
    nn, nt, tn = ((((1,), (0,)), ((), ())), (((1,), (1,)), ((), ())), (((0,), (0,)), ((), ())))
    corner = gram[:half, half:] + gram[half:, :half].T
    work[...] = gram[:half, :half]
    factor[half:, :half] = jnp.zeros((half, half), f32)
    inv[:half, half:] = jnp.zeros((half, half), f32)

    @pl.loop(0, 2)
    def _(i):
        eliminate(work, up.at[i], low.at[i])

        @pl.when(i == 0)
        def _():
            across = exact(low[0], corner, nn)
            factor[:half, half:] = across * (1.0 / root)
            work[...] = gram[half:, half:] - exact(across, across, tn)

    across = factor[:half, half:] * root
    inv[:half, :half] = low[0]
    inv[half:, half:] = low[1]
    inv[half:, :half] = -exact(low[1], exact(across, low[0], tn), nn)
    factor[:half, :half] = up[0] * (1.0 / root)
    factor[half:, half:] = up[1] * (1.0 / root)

    mine = inv[pl.ds(pl.multiple_of(col[0] * width, width), width), :] * root
    high = mine.astype(bf16)
    rest = mine - high.astype(f32)
    mid = rest.astype(bf16)
    last = (rest - mid.astype(f32)).astype(bf16)
    left = jnp.concatenate([high, mid, last], axis=0)

    fetch.wait()
    for k in range(lb):
        right = jnp.concatenate([whole[q, k] for q in range(parts)], axis=0)
        r = jnp.dot(left, right, preferred_element_type=f32)
        basis[:, k * bs:(k + 1) * bs] = r[:width] + (r[width:2 * width] + r[2 * width:])


def body(subspace, onsite, blocks, cols):
    row_count = lax.axis_size("row")
    part_width, local_rows = subspace.shape
    whole, gram = filtered(subspace, onsite, blocks, cols)
    full = gram.shape[0]
    half = full // 2
    root = math.sqrt(row_count * local_rows)
    vm = pltpu.VMEM
    return pl.pallas_call(
        functools.partial(finish_kernel, root),
        out_shape=(jax.ShapeDtypeStruct((part_width, local_rows), f32),
                   jax.ShapeDtypeStruct((full, full), f32)),
        in_specs=[pl.BlockSpec(memory_space=pltpu.SMEM), pl.BlockSpec(memory_space=pltpu.HBM),
                  pl.BlockSpec(memory_space=vm)],
        out_specs=[pl.BlockSpec(memory_space=vm)] * 2,
        scratch_shapes=[vm((half, half), f32), vm((2, half, half), f32), vm((2, half, half), f32),
                        vm((full, full), f32), vm(whole.shape, bf16), pltpu.SemaphoreType.DMA],
        compiler_params=pltpu.CompilerParams(vmem_limit_bytes=60 * 1024 * 1024),
        name="finish",
    )(lax.axis_index("col").astype(jnp.int32).reshape(1), whole, gram)


def solution(mesh):
    in_specs = (P("col", "row"), P("row"), P(None, "row", None, None), P())
    out_specs = (P("col", "row"), P())
    return jax.shard_map(body, mesh=mesh, in_specs=in_specs, out_specs=out_specs, check_vma=False)
```

```python
import functools
import math

import jax
import jax.numpy as jnp
from jax import lax
from jax.experimental import pallas as pl
from jax.experimental.pallas import tpu as pltpu
from jax.sharding import PartitionSpec as P

HALO = 4
FILTER = 4
UNROLL = 4
HALVES = 1
filter_scale = 0.4
f32 = jnp.float32
bf16 = jnp.bfloat16


def shifts_of(rows):
    return (rows // 2, 2, 1, -1)


def bits_below(k):
    return lax.shift_left(jnp.ones_like(k), k) - 1


def ones_in(x):
    return lax.population_count(x)


def folded(x, axis):
    step = x.shape[axis] // 2
    while step:
        x = x | pltpu.roll(x, step, axis)
        step //= 2
    return x


def tiles_of(sc):
    return list(range(0, sc - 7, 8)) + ([sc - 8] if sc % 8 else [])


def masks_of(cvm, rows, me, lb, sc):
    shifts = shifts_of(rows)
    groups = len(shifts)
    lane = lax.broadcasted_iota(jnp.int32, (8, 128), 1)
    sub = lax.broadcasted_iota(jnp.int32, (8, 128), 0)
    per = 128 // lb

    def picked(device, owners):
        start = pl.multiple_of(device // per * 128, 128)
        live = lane // lb == lax.rem(device, per)
        found = [jnp.zeros((8, 128), jnp.int32) for _ in owners]
        for o in tiles_of(sc):
            v = cvm[o:o + 8, pl.ds(start, 128)]
            for n, owner in enumerate(owners):
                rel = v - owner * lb
                hit = live & (rel >= 0) & (rel < lb)
                found[n] = found[n] | jnp.where(
                    hit, lax.shift_left(jnp.ones_like(rel), rel & (lb - 1)), 0)
        return found

    found = picked(me, [lax.rem(me + d + rows, rows) for d in shifts])
    for d in shifts:
        found += picked(lax.rem(me - d + rows, rows), [me])
    both = jnp.zeros((8, 128), jnp.int32)
    for n, x in enumerate(found):
        both = jnp.where(sub == n, folded(x, 0), both)
    assert groups == 4
    return folded(both, 1)


def mask_row(masks, n):
    return jnp.broadcast_to(masks[n:n + 1, :], (8, 128))


def byte_of(word, n, limit):
    return lax.shift_right_logical(word, 8 * n) & (limit - 1)


def packed_exports(masks, lb, names):
    k = lax.broadcasted_iota(jnp.int32, (8, 128), 1)
    low = jnp.minimum(k, lb - 1)
    hit = (k < lb) & ((lax.shift_right_logical(masks, low) & 1) == 1)
    rank = ones_in(masks & bits_below(low))
    word = jnp.zeros((8, 128), jnp.int32)
    for m in range(HALO):
        word = word | jnp.where(hit & (rank == m), lax.shift_left(names, jnp.full_like(names, 8 * m)), 0)
    return folded(word, 1)


def order_of(masks, groups, at):
    taken = jnp.zeros((8, 128), jnp.int32)
    base = jnp.zeros((8, 128), jnp.int32)
    place = jnp.zeros((8, 128), jnp.int32)
    below = bits_below(at)
    for g in range(groups + 1):
        left = ~taken
        mine = left if g == groups else mask_row(masks, groups + g) & left
        here = (lax.shift_right_logical(mine, at) & 1) == 1
        place = jnp.where(here, base + ones_in(mine & below), place)
        base = base + ones_in(mine)
        taken = taken | mine
    return place


def flip(c, bit):
    return c + bit - 2 * bit * lax.rem(c // bit, 2)


def hops_of(parts):
    hops, held, bit = [], [0], parts // 2
    while bit:
        hops += [(bit, m) for m in held]
        held += [m + bit for m in held]
        bit //= 2
    return hops


def slice_of(width, rows):
    return max(8, width // rows)


def filter_kernel(rows, parts, lb, sc, cols, sub, ons_in, blk, stored, gram, bm, *refs):
    refs = list(refs)
    take = lambda n: [refs.pop(0) for _ in range(n)]
    halves = range(HALVES)
    xs = [take(HALVES) for _ in range(FILTER)]
    snds = [take(HALVES) for _ in range(FILTER)]
    ys = [take(HALVES) for _ in range(FILTER - 1)]
    s0 = take(HALVES)
    (out, ons, cvm, early_v, late_v, early, late, gp, gs, rb, bsem, xsem, csem, ssem, rsem,
     wss, wrs, pss, prs, ass, ars, tsem, osem) = refs
    me = lax.axis_index("row")
    mc = lax.axis_index("col")
    everyone = rows * parts
    linear = me * parts + mc
    width = sub.shape[0]
    hw = width // HALVES
    hops = hops_of(parts)
    rps = slice_of(width, rows)
    reducers = width // rps
    shifts = shifts_of(rows)
    groups = len(shifts)
    bs = blk.shape[-1]
    chunks = lb // UNROLL

    def load(c):
        part = pl.ds(c * UNROLL, UNROLL)
        return pltpu.make_async_copy(blk.at[:, part], bm.at[:, part], bsem.at[c])

    def first(i, h):
        cut = sub.at[pl.ds(h * hw, hw), pl.ds(pl.multiple_of(i * bs, bs), bs)]
        return (pltpu.make_async_copy(cut, xs[0][h].at[i], xsem.at[h, i]),
                pltpu.make_async_copy(cut, s0[h].at[i], csem.at[h, i]))

    barrier = pltpu.get_barrier_semaphore()

    @pl.loop(1, everyone)
    def _(e):
        to = lax.rem(linear + e, everyone)
        pl.semaphore_signal(barrier, inc=1, device_id=(to // parts, lax.rem(to, parts)),
                            device_id_type=pl.DeviceIdType.MESH)

    named = pltpu.make_async_copy(cols, cvm, tsem.at[0])
    named.start()
    for h in halves:
        @pl.loop(0, lb)
        def _(i):
            a, b = first(i, h)
            b.start()
            a.start()

    energies = pltpu.make_async_copy(ons_in, ons, tsem.at[1])
    energies.start()

    @pl.loop(0, chunks)
    def _(c):
        load(c).start()

    named.wait()
    masks = masks_of(cvm, rows, me, lb, sc)
    lane = lax.broadcasted_iota(jnp.int32, (8, 128), 1)
    sublane = lax.broadcasted_iota(jnp.int32, (8, 128), 0)
    early_v[...] = packed_exports(masks, lb, lane)
    to_early = pltpu.make_async_copy(early_v, early, tsem.at[2])
    to_early.start()

    inverse = order_of(masks, groups, jnp.minimum(lane, lb - 1))
    late_v[0:8, :] = packed_exports(masks, lb, inverse)
    word = jnp.zeros((8, 128), jnp.int32)
    for q in range(lb // 8):
        word = word | jnp.where((lane < lb) & (inverse == 8 * q + sublane),
                                lax.shift_left(lane, jnp.full_like(lane, 8 * q)), 0)
    late_v[8:16, :] = folded(word, 1)
    late_v[16:24, :] = inverse
    per = 128 // lb
    start = pl.multiple_of(me // per * 128, 128)
    for o in tiles_of(sc):
        v = cvm[o:o + 8, pl.ds(start, 128)]
        rel = v - me * lb
        near = (rel >= 0) & (rel < lb)
        low = rel & (lb - 1)
        far = jnp.zeros((8, 128), jnp.int32)
        for g, d in enumerate(shifts):
            there = v - lax.rem(me + d + rows, rows) * lb
            at = there & (lb - 1)
            far = jnp.where((there >= 0) & (there < lb),
                            lb + HALO * g + ones_in(mask_row(masks, g) & bits_below(at)), far)
        late_v[24 + o:32 + o, :] = jnp.where(near, low, far)
        late_v[24 + sc + o:32 + sc + o, :] = jnp.where(near, order_of(masks, groups, low), far)
    to_late = pltpu.make_async_copy(late_v, late, tsem.at[3])
    shift = lax.rem(me, per) * lb
    pn, pp, span = 24, 24 + sc, xs[0][0].shape[0]

    def export(k, g, m):
        return byte_of(early[groups + g, 0] if k == 0 else late[groups + g, 0], m, lb)

    def permuted(j):
        return byte_of(late[8 + lax.rem(j, 8), 0], j // 8, lb)

    def copy(k, h, g):
        return pltpu.make_async_remote_copy(
            src_ref=snds[k][h].at[pl.ds(g * HALO, HALO)],
            dst_ref=xs[k][h].at[pl.ds(lb + g * HALO, HALO)],
            send_sem=ssem.at[k, h, g], recv_sem=rsem.at[k, h, g],
            device_id=(lax.rem(me - shifts[g] + rows, rows), mc),
            device_id_type=pl.DeviceIdType.MESH)

    def pack(k, h, g, source):
        for m in range(HALO):
            snds[k][h][g * HALO + m] = source[export(k, g, m)].astype(bf16)

    for h in halves:
        @pl.loop(0, lb)
        def _(i):
            first(i, h)[1].wait()

        to_early.wait()
        for g in range(groups):
            pack(0, h, g, s0[h])
        if h == 0:
            pl.semaphore_wait(barrier, everyone - 1)
        for g in range(groups):
            copy(0, h, g).start()

    to_late.start()
    for h in halves:
        @pl.loop(0, lb)
        def _(i):
            first(i, h)[0].wait()

    energies.wait()
    to_late.wait()

    def place(k, j):
        i = j if k == FILTER - 1 else permuted(j)
        own = late[16, j] & (lb - 1) if k == FILTER - 1 else (i if k == 0 else j)
        return i, own

    def feed(k, first_row, accs):
        base = pn if k == 0 else pp
        x = xs[k][0]
        at = [place(k, first_row + u)[0] for u in range(UNROLL)]
        for t in range(sc // 2):
            for m in range(2):
                pair = at[2 * m:2 * m + 2]
                pltpu.matmul_push_rhs(jnp.concatenate(
                    [jnp.concatenate([bm[2 * t, i], bm[2 * t + 1, i]], axis=0) for i in pair],
                    axis=1), t % 2, m)
                for u, i in enumerate(pair):
                    left = jnp.concatenate(
                        [x[late[base + 2 * t + s, shift + i] & (span - 1)] for s in range(2)], axis=1)
                    pltpu.matmul_acc_lhs(accs[m][u], left,
                                         load_staged_rhs=t % 2 if u == 0 else None)

    def settle(k, row, acc, u):
        i, own = place(k, row)
        total = pltpu.matmul_pop(acc)[:, u * bs:(u + 1) * bs]
        total = total + ons[i] * xs[k][0][own].astype(f32)
        if k == 0:
            return filter_scale * total
        prev = xs[0][0][i].astype(f32) if k == 1 else ys[k - 2][0][own]
        return 2.0 * filter_scale * total - prev

    def turn(piece, c):
        return lax.rem(c + (1 - piece // (parts // 2)) * (chunks // 2), chunks)

    def spread(n, h, c):
        bit, m = hops[n]
        piece = mc
        for b in (m & (1 << t) for t in range(m.bit_length())):
            if b:
                piece = flip(piece, b)
        part = out.at[piece * HALVES + h, pl.ds(turn(piece, c) * UNROLL, UNROLL)]
        return pltpu.make_async_remote_copy(
            src_ref=part, dst_ref=part, send_sem=wss.at[n, h, c], recv_sem=wrs.at[n, h, c],
            device_id=(me, flip(mc, bit)), device_id_type=pl.DeviceIdType.MESH)

    firsts = [n for n, (_, m) in enumerate(hops) if m == 0]

    @pl.loop(0, chunks)
    def _(c):
        load(c).wait()

    def keep(k, j, value):
        low = value.astype(bf16)
        if k < FILTER - 1:
            xs[k + 1][0][j] = low
            ys[k][0][j] = value
        else:
            out[mc, j] = low

    def rows_of(k, c):
        return (turn(mc, c) if k == FILTER - 1 else c) * UNROLL

    def chunk(k, c, accs):
        for m in range(2):
            for u in range(2):
                j = rows_of(k, c) + 2 * m + u
                keep(k, j, settle(k, j, accs[m][u], u))

    def filtering(*flat):
        sets = [[flat[4 * q + 2 * m:4 * q + 2 * m + 2] for m in range(2)] for q in range(2)]
        for k in range(FILTER):
            for g in range(groups):
                copy(k, 0, g).wait_recv()
            ahead = groups if k < FILTER - 1 else 0
            for c in range(0, ahead, 2):
                for q in range(2):
                    feed(k, rows_of(k, c + q), sets[q])
                if c:
                    copy(k + 1, 0, c - 1).start()
                for q in range(2):
                    chunk(k, c + q, sets[q])
                    if q:
                        copy(k + 1, 0, c).start()
                    pack(k + 1, 0, c + q, ys[k][0])

            @pl.loop(ahead // 2, chunks // 2)
            def _(cc):
                for q in range(2):
                    feed(k, rows_of(k, 2 * cc + q), sets[q])
                if ahead:
                    @pl.when(cc == ahead // 2)
                    def _():
                        copy(k + 1, 0, ahead - 1).start()
                for q in range(2):
                    chunk(k, 2 * cc + q, sets[q])
                if k == FILTER - 1:
                    @pl.when(cc > 0)
                    def _():
                        for n in firsts:
                            for q in range(2):
                                spread(n, 0, 2 * cc - 2 + q).start()
            if k == FILTER - 1:
                for n in firsts:
                    for q in range(2):
                        spread(n, 0, chunks - 2 + q).start()

    pl.run_scoped(filtering, *[pltpu.ACC(m)((width, 2 * bs), f32)
                               for _ in range(2) for m in range(2) for _ in range(2)])

    for k in range(FILTER):
        for h in halves:
            for g in range(groups):
                copy(k, h, g).wait_send()

    needs = {n: max(q for q in range(n) if sum(hops[q]) == m)
             for n, (_, m) in enumerate(hops) if m}
    def relay(lo, hi):
        for h in halves:
            @pl.loop(lo, hi)
            def _(c):
                got = set()
                for n in needs:
                    if needs[n] not in got:
                        spread(needs[n], h, c).wait_recv()
                        got.add(needs[n])
                    spread(n, h, c).start()

    def arrive(lo, hi, picked):
        for h in halves:
            @pl.loop(lo, hi)
            def _(c):
                for n in picked:
                    spread(n, h, c).wait_recv()

    top = parts // 2
    leaves = [n for n in range(len(hops)) if n not in needs.values()]
    near = [n for n in leaves if sum(hops[n]) < top]
    other = [n for n in leaves if sum(hops[n]) >= top]
    relay(0, chunks // 2)
    arrive(0, chunks, near)
    arrive(0, chunks // 2, other)

    side = mc // top
    half = lb // 2

    def tall(q, first_row):
        return jnp.concatenate([out[q, first_row], out[q, first_row + 1]], axis=1)

    def gramming(*accs):
        both, one, two = [accs[2 * n:2 * n + 2] for n in range(3)]

        @pl.loop(0, half // 4)
        def _(c):
            for m in range(2):
                row = side * half + c * 4 + 2 * m
                pltpu.matmul_push_rhs(
                    jnp.concatenate([tall(q, row) for q in range(parts)], axis=0),
                    0, m, transpose=True)
                pltpu.matmul_acc_lhs(both[m], tall(mc, row), load_staged_rhs=0)

        @pl.loop(0, half // 8)
        def _(c):
            for m in range(2):
                row = (1 - side) * half + c * 8 + 4 * m
                pltpu.matmul_push_rhs(
                    jnp.concatenate([tall(side * top + q, row + r)
                                     for r in (0, 2) for q in range(top)], axis=0),
                    0, m, transpose=True)
                pltpu.matmul_acc_lhs(one[m], tall(mc, row), load_staged_rhs=0)
                pltpu.matmul_acc_lhs(two[m], tall(mc, row + 2))

        across = top * width
        gp[...] = pltpu.matmul_pop(both[0]) + pltpu.matmul_pop(both[1])
        cut = pl.ds(pl.multiple_of(side * across, across), across)
        near_sum = [pltpu.matmul_pop(one[m])[:, :across] + pltpu.matmul_pop(two[m])[:, across:]
                    for m in range(2)]
        gp[:, cut] += near_sum[0] + near_sum[1]

    pl.run_scoped(gramming, *[pltpu.ACC(m)((width, parts * width), f32)
                              for _ in range(3) for m in range(2)])

    def part_to(d):
        to = lax.rem(me + d, rows)
        lo = pl.multiple_of(to * rps, rps)
        return to, pltpu.make_async_remote_copy(
            src_ref=gp.at[pl.ds(lo, rps)], dst_ref=rb.at[d], send_sem=pss.at[d],
            recv_sem=prs.at[d], device_id=(to, mc), device_id_type=pl.DeviceIdType.MESH)

    def part_in(d):
        return pltpu.make_async_remote_copy(
            src_ref=gp.at[pl.ds(0, rps)], dst_ref=rb.at[d], send_sem=pss.at[d],
            recv_sem=prs.at[d], device_id=(lax.rem(me + 1, rows), mc),
            device_id_type=pl.DeviceIdType.MESH)

    def only(cond, run):
        if reducers == rows:
            run()
        else:
            pl.when(cond)(run)

    @pl.loop(1, rows)
    def _(d):
        to, c = part_to(d)
        only(to < reducers, lambda: c.start())

    def all_to(e, sender):
        to = lax.rem(linear + e, everyone)
        lo = pl.multiple_of((lax.rem(sender, parts) * reducers + sender // parts) * rps, rps)
        return pltpu.make_async_remote_copy(
            src_ref=gs, dst_ref=gram.at[pl.ds(lo, rps)], send_sem=ass.at[e],
            recv_sem=ars.at[e], device_id=(to // parts, lax.rem(to, parts)),
            device_id_type=pl.DeviceIdType.MESH)

    def reduce():
        lo = pl.multiple_of(me * rps, rps)
        total = gp[pl.ds(lo, rps)]
        for d in range(1, rows):
            part_in(d).wait_recv()
            total = total + rb[d]
        gs[...] = total
        gram[pl.ds(pl.multiple_of((mc * reducers + me) * rps, rps), rps)] = total

        @pl.loop(1, everyone)
        def _(e):
            all_to(e, linear).start()

    only(me < reducers, reduce)
    relay(chunks // 2, chunks)
    arrive(chunks // 2, chunks, other)
    keep_all = pltpu.make_async_copy(out, stored, osem)
    keep_all.start()
    for h in halves:
        @pl.loop(0, chunks)
        def _(c):
            for n in range(len(hops)):
                spread(n, h, c).wait_send()

    @pl.loop(1, rows)
    def _(d):
        to, c = part_to(d)
        only(to < reducers, lambda: c.wait_send())

    @pl.loop(1, everyone)
    def _(e):
        sender = lax.rem(linear - e + everyone, everyone)
        only(me < reducers, lambda: all_to(e, linear).wait_send())
        only(sender // parts < reducers, lambda: all_to(e, sender).wait_recv())
    keep_all.wait()


def filtered(subspace, onsite, blocks, cols):
    rows, parts = lax.axis_size("row"), lax.axis_size("col")
    everyone, hops = rows * parts, len(hops_of(parts))
    width = subspace.shape[0]
    sc, lb, bs, _ = blocks.shape
    groups = len(shifts_of(rows))
    assert lb in (8, 16, 32) and sc >= 8
    ext = pl.next_power_of_2(lb + groups * HALO)
    vm, dma = pltpu.VMEM, pltpu.SemaphoreType.DMA
    full, hw = parts * width, width // HALVES
    rps = slice_of(width, rows)
    return pl.pallas_call(
        functools.partial(filter_kernel, rows, parts, lb, sc),
        out_shape=(jax.ShapeDtypeStruct((parts * HALVES, lb, hw, bs), bf16),
                   jax.ShapeDtypeStruct((full, full), f32)),
        in_specs=[pl.BlockSpec(memory_space=pl.ANY)] * 4,
        out_specs=[pl.BlockSpec(memory_space=pl.ANY), pl.BlockSpec(memory_space=vm)],
        scratch_shapes=[vm((sc, lb, bs, bs), bf16)]
        + [vm((ext, hw, bs), bf16)] * (FILTER * HALVES)
        + [vm((groups * HALO, hw, bs), bf16)] * (FILTER * HALVES)
        + [vm((lb, hw, bs), f32)] * ((FILTER - 1) * HALVES)
        + [vm((lb, hw, bs), bf16)] * HALVES
        + [vm((parts * HALVES, lb, hw, bs), bf16), vm((lb, 1, bs), f32), vm(cols.shape[::-1], jnp.int32),
           vm((8, 128), jnp.int32), vm((24 + 2 * sc, 128), jnp.int32),
           pltpu.SMEM((8, 128), jnp.int32), pltpu.SMEM((24 + 2 * sc, 128), jnp.int32)]
        + [vm((width, full), f32), vm((rps, full), f32), vm((rows, rps, full), f32)]
        + [dma((lb // UNROLL,)), dma((HALVES, lb)), dma((HALVES, lb)),
           dma((FILTER, HALVES, groups)), dma((FILTER, HALVES, groups)),
           dma((hops, HALVES, lb // UNROLL)), dma((hops, HALVES, lb // UNROLL)),
           dma((rows,)), dma((rows,)), dma((everyone,)), dma((everyone,)), dma((4,)), dma],
        compiler_params=pltpu.CompilerParams(
            collective_id=0, has_side_effects=True, vmem_limit_bytes=56 * 1024 * 1024),
        name="filter",
    )(cols.T, subspace, onsite.reshape(lb, 1, bs), blocks)


def eliminate(src, up, low):
    n = src.shape[0]
    tiles = n // 8
    a = [src[8 * t:8 * t + 8, :] for t in range(tiles)]
    sub = lax.broadcasted_iota(jnp.int32, (8, n), 0)
    lane = lax.broadcasted_iota(jnp.int32, (8, n), 1)
    b = [jnp.where(lane == sub + 8 * t, 1.0, 0.0).astype(f32) for t in range(tiles)]

    def row(v, q):
        return jnp.broadcast_to(v[q:q + 1, :], (8, n))

    for p in range(tiles):
        cols = {t: [jnp.broadcast_to(a[t][:, 8 * p + q:8 * p + q + 1], (8, n)) for q in range(8)]
                for t in range(p, tiles)}
        pivots = jnp.ones((8, n), f32)
        for q in range(8):
            pivot = row(cols[p][q], q)
            pivots = jnp.where(sub == q, pivot, pivots)
            inverse = 1.0 / pivot
            right = [row(cols[p][k], q) for k in range(8)]
            arow, brow = row(a[p], q), row(b[p], q)
            for t in range(p, tiles):
                m = cols[t][q] * inverse
                if t == p:
                    m = jnp.where(sub > q, m, 0.0)
                for k in range(q + 1, 8):
                    cols[t][k] = cols[t][k] - m * right[k]
                a[t] = a[t] - m * arow
                b[t] = b[t] - m * brow
        scale = lax.rsqrt(pivots)
        up[8 * p:8 * p + 8, :] = jnp.where(lane >= sub + 8 * p, a[p] * scale, 0.0)
        low[8 * p:8 * p + 8, :] = b[p] * scale


def finish_kernel(root, col, stored, gram, basis, factor, work, up, low, inv, whole, sem):
    fetch = pltpu.make_async_copy(stored, whole, sem)
    fetch.start()
    parts, lb, _, bs = whole.shape
    width = basis.shape[0]
    full = gram.shape[0]
    half = full // 2
    exact = functools.partial(lax.dot_general, precision=lax.Precision.HIGHEST,
                              preferred_element_type=f32)
    nn, nt, tn = ((((1,), (0,)), ((), ())), (((1,), (1,)), ((), ())), (((0,), (0,)), ((), ())))
    corner = gram[:half, half:] + gram[half:, :half].T
    work[...] = gram[:half, :half]
    factor[half:, :half] = jnp.zeros((half, half), f32)
    inv[:half, half:] = jnp.zeros((half, half), f32)

    @pl.loop(0, 2)
    def _(i):
        eliminate(work, up.at[i], low.at[i])

        @pl.when(i == 0)
        def _():
            across = exact(low[0], corner, nn)
            factor[:half, half:] = across * (1.0 / root)
            work[...] = gram[half:, half:] - exact(across, across, tn)

    across = factor[:half, half:] * root
    inv[:half, :half] = low[0]
    inv[half:, half:] = low[1]
    inv[half:, :half] = -exact(low[1], exact(across, low[0], tn), nn)
    factor[:half, :half] = up[0] * (1.0 / root)
    factor[half:, half:] = up[1] * (1.0 / root)

    mine = inv[pl.ds(pl.multiple_of(col[0] * width, width), width), :] * root
    high = mine.astype(bf16)
    rest = mine - high.astype(f32)
    mid = rest.astype(bf16)
    last = (rest - mid.astype(f32)).astype(bf16)
    left = jnp.concatenate([high, mid, last], axis=0)

    fetch.wait()
    for k in range(lb):
        right = jnp.concatenate([whole[q, k] for q in range(parts)], axis=0)
        r = jnp.dot(left, right, preferred_element_type=f32)
        basis[:, k * bs:(k + 1) * bs] = r[:width] + (r[width:2 * width] + r[2 * width:])


def body(subspace, onsite, blocks, cols):
    row_count = lax.axis_size("row")
    part_width, local_rows = subspace.shape
    whole, gram = filtered(subspace, onsite, blocks, cols)
    full = gram.shape[0]
    half = full // 2
    root = math.sqrt(row_count * local_rows)
    vm = pltpu.VMEM
    return pl.pallas_call(
        functools.partial(finish_kernel, root),
        out_shape=(jax.ShapeDtypeStruct((part_width, local_rows), f32),
                   jax.ShapeDtypeStruct((full, full), f32)),
        in_specs=[pl.BlockSpec(memory_space=pltpu.SMEM), pl.BlockSpec(memory_space=pltpu.HBM),
                  pl.BlockSpec(memory_space=vm)],
        out_specs=[pl.BlockSpec(memory_space=vm)] * 2,
        scratch_shapes=[vm((half, half), f32), vm((2, half, half), f32), vm((2, half, half), f32),
                        vm((full, full), f32), vm(whole.shape, bf16), pltpu.SemaphoreType.DMA],
        compiler_params=pltpu.CompilerParams(vmem_limit_bytes=60 * 1024 * 1024),
        name="finish",
    )(lax.axis_index("col").astype(jnp.int32).reshape(1), whole, gram)


def solution(mesh):
    in_specs = (P("col", "row"), P("row"), P(None, "row", None, None), P())
    out_specs = (P("col", "row"), P())
    return jax.shard_map(body, mesh=mesh, in_specs=in_specs, out_specs=out_specs, check_vma=False)
```

```python
import functools
import math

import jax
import jax.numpy as jnp
from jax import lax
from jax.experimental import pallas as pl
from jax.experimental.pallas import tpu as pltpu
from jax.sharding import PartitionSpec as P

HALO = 4
FILTER = 4
UNROLL = 4
HALVES = 1
filter_scale = 0.4
f32 = jnp.float32
bf16 = jnp.bfloat16


def shifts_of(rows):
    return (rows // 2, 2, 1, -1)


def bits_below(k):
    return lax.shift_left(jnp.ones_like(k), k) - 1


def ones_in(x):
    return lax.population_count(x)


def folded(x, axis):
    step = x.shape[axis] // 2
    while step:
        x = x | pltpu.roll(x, step, axis)
        step //= 2
    return x


def tiles_of(sc):
    return list(range(0, sc - 7, 8)) + ([sc - 8] if sc % 8 else [])


def masks_of(cvm, rows, me, lb, sc):
    shifts = shifts_of(rows)
    groups = len(shifts)
    lane = lax.broadcasted_iota(jnp.int32, (8, 128), 1)
    sub = lax.broadcasted_iota(jnp.int32, (8, 128), 0)
    per = 128 // lb

    def picked(device, owners):
        start = pl.multiple_of(device // per * 128, 128)
        live = lane // lb == lax.rem(device, per)
        found = [jnp.zeros((8, 128), jnp.int32) for _ in owners]
        for o in tiles_of(sc):
            v = cvm[o:o + 8, pl.ds(start, 128)]
            for n, owner in enumerate(owners):
                rel = v - owner * lb
                hit = live & (rel >= 0) & (rel < lb)
                found[n] = found[n] | jnp.where(
                    hit, lax.shift_left(jnp.ones_like(rel), rel & (lb - 1)), 0)
        return found

    found = picked(me, [lax.rem(me + d + rows, rows) for d in shifts])
    for d in shifts:
        found += picked(lax.rem(me - d + rows, rows), [me])
    both = jnp.zeros((8, 128), jnp.int32)
    for n, x in enumerate(found):
        both = jnp.where(sub == n, folded(x, 0), both)
    assert groups == 4
    return folded(both, 1)


def mask_row(masks, n):
    return jnp.broadcast_to(masks[n:n + 1, :], (8, 128))


def byte_of(word, n, limit):
    return lax.shift_right_logical(word, 8 * n) & (limit - 1)


def packed_exports(masks, lb, names):
    k = lax.broadcasted_iota(jnp.int32, (8, 128), 1)
    low = jnp.minimum(k, lb - 1)
    hit = (k < lb) & ((lax.shift_right_logical(masks, low) & 1) == 1)
    rank = ones_in(masks & bits_below(low))
    word = jnp.zeros((8, 128), jnp.int32)
    for m in range(HALO):
        word = word | jnp.where(hit & (rank == m), lax.shift_left(names, jnp.full_like(names, 8 * m)), 0)
    return folded(word, 1)


def order_of(masks, groups, at):
    taken = jnp.zeros((8, 128), jnp.int32)
    base = jnp.zeros((8, 128), jnp.int32)
    place = jnp.zeros((8, 128), jnp.int32)
    below = bits_below(at)
    for g in range(groups + 1):
        left = ~taken
        mine = left if g == groups else mask_row(masks, groups + g) & left
        here = (lax.shift_right_logical(mine, at) & 1) == 1
        place = jnp.where(here, base + ones_in(mine & below), place)
        base = base + ones_in(mine)
        taken = taken | mine
    return place


def flip(c, bit):
    return c + bit - 2 * bit * lax.rem(c // bit, 2)


def hops_of(parts):
    hops, held, bit = [], [0], parts // 2
    while bit:
        hops += [(bit, m) for m in held]
        held += [m + bit for m in held]
        bit //= 2
    return hops


def slice_of(width, rows):
    return max(8, width // rows)


def filter_kernel(rows, parts, lb, sc, cols, sub, ons_in, blk, stored, gram, first_up,
                  first_low, bm, *refs):
    refs = list(refs)
    take = lambda n: [refs.pop(0) for _ in range(n)]
    halves = range(HALVES)
    xs = [take(HALVES) for _ in range(FILTER)]
    snds = [take(HALVES) for _ in range(FILTER)]
    ys = [take(HALVES) for _ in range(FILTER - 1)]
    s0 = take(HALVES)
    (out, ons, cvm, early_v, late_v, early, late, gp, gs, rb, bsem, xsem, csem, ssem, rsem,
     wss, wrs, pss, prs, ass, ars, tsem, osem) = refs
    me = lax.axis_index("row")
    mc = lax.axis_index("col")
    everyone = rows * parts
    linear = me * parts + mc
    width = sub.shape[0]
    hw = width // HALVES
    hops = hops_of(parts)
    rps = slice_of(width, rows)
    reducers = width // rps
    shifts = shifts_of(rows)
    groups = len(shifts)
    bs = blk.shape[-1]
    chunks = lb // UNROLL

    def load(c):
        part = pl.ds(c * UNROLL, UNROLL)
        return pltpu.make_async_copy(blk.at[:, part], bm.at[:, part], bsem.at[c])

    def first(i, h):
        cut = sub.at[pl.ds(h * hw, hw), pl.ds(pl.multiple_of(i * bs, bs), bs)]
        return (pltpu.make_async_copy(cut, xs[0][h].at[i], xsem.at[h, i]),
                pltpu.make_async_copy(cut, s0[h].at[i], csem.at[h, i]))

    barrier = pltpu.get_barrier_semaphore()

    @pl.loop(1, everyone)
    def _(e):
        to = lax.rem(linear + e, everyone)
        pl.semaphore_signal(barrier, inc=1, device_id=(to // parts, lax.rem(to, parts)),
                            device_id_type=pl.DeviceIdType.MESH)

    named = pltpu.make_async_copy(cols, cvm, tsem.at[0])
    named.start()
    for h in halves:
        @pl.loop(0, lb)
        def _(i):
            a, b = first(i, h)
            b.start()
            a.start()

    energies = pltpu.make_async_copy(ons_in, ons, tsem.at[1])
    energies.start()

    @pl.loop(0, chunks)
    def _(c):
        load(c).start()

    named.wait()
    masks = masks_of(cvm, rows, me, lb, sc)
    lane = lax.broadcasted_iota(jnp.int32, (8, 128), 1)
    sublane = lax.broadcasted_iota(jnp.int32, (8, 128), 0)
    early_v[...] = packed_exports(masks, lb, lane)
    to_early = pltpu.make_async_copy(early_v, early, tsem.at[2])
    to_early.start()

    to_late = pltpu.make_async_copy(late_v, late, tsem.at[3])
    shift = lax.rem(me, 128 // lb) * lb
    pn, pp, span = 24, 24 + sc, xs[0][0].shape[0]

    def export(k, g, m):
        return byte_of(early[groups + g, 0] if k == 0 else late[groups + g, 0], m, lb)

    def permuted(j):
        return byte_of(late[8 + lax.rem(j, 8), 0], j // 8, lb)

    def offset_of(g):
        if isinstance(g, int):
            return shifts[g]
        found = shifts[-1]
        for n in range(groups - 1):
            found = jnp.where(g == n, shifts[n], found)
        return found

    def copy(k, h, g):
        return pltpu.make_async_remote_copy(
            src_ref=snds[k][h].at[pl.ds(g * HALO, HALO)],
            dst_ref=xs[k][h].at[pl.ds(lb + g * HALO, HALO)],
            send_sem=ssem.at[k, h, g], recv_sem=rsem.at[k, h, g],
            device_id=(lax.rem(me - offset_of(g) + rows, rows), mc),
            device_id_type=pl.DeviceIdType.MESH)

    def pack(k, h, g, source):
        for m in range(HALO):
            snds[k][h][g * HALO + m] = source[export(k, g, m)].astype(bf16)

    for h in halves:
        @pl.loop(0, lb)
        def _(i):
            first(i, h)[1].wait()

        to_early.wait()
        for g in range(groups):
            pack(0, h, g, s0[h])
        if h == 0:
            pl.semaphore_wait(barrier, everyone - 1)
        for g in range(groups):
            copy(0, h, g).start()

    inverse = order_of(masks, groups, jnp.minimum(lane, lb - 1))
    late_v[0:8, :] = packed_exports(masks, lb, inverse)
    word = jnp.zeros((8, 128), jnp.int32)
    for q in range(lb // 8):
        word = word | jnp.where((lane < lb) & (inverse == 8 * q + sublane),
                                lax.shift_left(lane, jnp.full_like(lane, 8 * q)), 0)
    late_v[8:16, :] = folded(word, 1)
    late_v[16:24, :] = inverse
    per = 128 // lb
    start = pl.multiple_of(me // per * 128, 128)
    for o in tiles_of(sc):
        v = cvm[o:o + 8, pl.ds(start, 128)]
        rel = v - me * lb
        near = (rel >= 0) & (rel < lb)
        low = rel & (lb - 1)
        far = jnp.zeros((8, 128), jnp.int32)
        for g, d in enumerate(shifts):
            there = v - lax.rem(me + d + rows, rows) * lb
            at = there & (lb - 1)
            far = jnp.where((there >= 0) & (there < lb),
                            lb + HALO * g + ones_in(mask_row(masks, g) & bits_below(at)), far)
        late_v[24 + o:32 + o, :] = jnp.where(near, low, far)
        late_v[24 + sc + o:32 + sc + o, :] = jnp.where(near, order_of(masks, groups, low), far)
    to_late.start()
    for h in halves:
        @pl.loop(0, lb)
        def _(i):
            first(i, h)[0].wait()

    energies.wait()
    to_late.wait()

    def place(k, j):
        i = j if k == FILTER - 1 else permuted(j)
        own = late[16, j] & (lb - 1) if k == FILTER - 1 else (i if k == 0 else j)
        return i, own

    def feed(k, first_row, accs):
        base = pn if k == 0 else pp
        x = xs[k][0]
        at = [place(k, first_row + u)[0] for u in range(UNROLL)]
        for t in range(sc // 2):
            for m in range(2):
                pair = at[2 * m:2 * m + 2]
                pltpu.matmul_push_rhs(jnp.concatenate(
                    [jnp.concatenate([bm[2 * t, i], bm[2 * t + 1, i]], axis=0) for i in pair],
                    axis=1), t % 2, m)
                for u, i in enumerate(pair):
                    left = jnp.concatenate(
                        [x[late[base + 2 * t + s, shift + i] & (span - 1)] for s in range(2)], axis=1)
                    pltpu.matmul_acc_lhs(accs[m][u], left,
                                         load_staged_rhs=t % 2 if u == 0 else None)

    def settle(k, row, acc, u):
        i, own = place(k, row)
        total = pltpu.matmul_pop(acc)[:, u * bs:(u + 1) * bs]
        total = total + ons[i] * xs[k][0][own].astype(f32)
        if k == 0:
            return filter_scale * total
        prev = xs[0][0][i].astype(f32) if k == 1 else ys[k - 2][0][own]
        return 2.0 * filter_scale * total - prev

    def turn(piece, c):
        return lax.rem(c + (1 - piece // (parts // 2)) * (chunks // 2), chunks)

    def spread(n, h, c):
        bit, m = hops[n]
        piece = mc
        for b in (m & (1 << t) for t in range(m.bit_length())):
            if b:
                piece = flip(piece, b)
        part = out.at[piece * HALVES + h, pl.ds(turn(piece, c) * UNROLL, UNROLL)]
        return pltpu.make_async_remote_copy(
            src_ref=part, dst_ref=part, send_sem=wss.at[n, h, c], recv_sem=wrs.at[n, h, c],
            device_id=(me, flip(mc, bit)), device_id_type=pl.DeviceIdType.MESH)

    firsts = [n for n, (_, m) in enumerate(hops) if m == 0]

    @pl.loop(0, chunks)
    def _(c):
        load(c).wait()

    def keep(k, j, value):
        low = value.astype(bf16)
        if k < FILTER - 1:
            xs[k + 1][0][j] = low
            ys[k][0][j] = value
        else:
            out[mc, j] = low

    def rows_of(k, c):
        return (turn(mc, c) if k == FILTER - 1 else c) * UNROLL

    def chunk(k, c, accs):
        for m in range(2):
            for u in range(2):
                j = rows_of(k, c) + 2 * m + u
                keep(k, j, settle(k, j, accs[m][u], u))

    def filtering(*flat):
        sets = [[flat[4 * q + 2 * m:4 * q + 2 * m + 2] for m in range(2)] for q in range(2)]
        for k in range(FILTER):
            for g in range(groups):
                copy(k, 0, g).wait_recv()
            last = k == FILTER - 1
            ahead = 0 if last else groups

            def eight(cc, send):
                for q in range(2):
                    feed(k, rows_of(k, 2 * cc + q), sets[q])
                if last:
                    @pl.when(cc > 0)
                    def _():
                        for n in firsts:
                            spread(n, 0, 2 * cc - 1).start()
                elif send:
                    @pl.when(cc > 0)
                    def _():
                        copy(k + 1, 0, 2 * cc - 1).start()
                else:
                    @pl.when(cc == ahead // 2)
                    def _():
                        copy(k + 1, 0, ahead - 1).start()
                chunk(k, 2 * cc, sets[0])
                if send:
                    pack(k + 1, 0, 2 * cc, ys[k][0])
                chunk(k, 2 * cc + 1, sets[1])
                if send:
                    copy(k + 1, 0, 2 * cc).start()
                    pack(k + 1, 0, 2 * cc + 1, ys[k][0])
                if last:
                    for n in firsts:
                        spread(n, 0, 2 * cc).start()

            if ahead:
                pl.loop(0, ahead // 2)(functools.partial(eight, send=True))
            pl.loop(ahead // 2, chunks // 2)(functools.partial(eight, send=False))
            if last:
                for n in firsts:
                    spread(n, 0, chunks - 1).start()

    pl.run_scoped(filtering, *[pltpu.ACC(m)((width, 2 * bs), f32)
                               for _ in range(2) for m in range(2) for _ in range(2)])

    for k in range(FILTER):
        for h in halves:
            for g in range(groups):
                copy(k, h, g).wait_send()

    needs = {n: max(q for q in range(n) if sum(hops[q]) == m)
             for n, (_, m) in enumerate(hops) if m}
    def relay(lo, hi):
        for h in halves:
            @pl.loop(lo, hi)
            def _(c):
                got = set()
                for n in needs:
                    if needs[n] not in got:
                        spread(needs[n], h, c).wait_recv()
                        got.add(needs[n])
                    spread(n, h, c).start()

    def arrive(lo, hi, picked):
        for h in halves:
            @pl.loop(lo, hi)
            def _(c):
                for n in picked:
                    spread(n, h, c).wait_recv()

    top = parts // 2
    leaves = [n for n in range(len(hops)) if n not in needs.values()]
    near = [n for n in leaves if sum(hops[n]) < top]
    other = [n for n in leaves if sum(hops[n]) >= top]
    side = mc // top
    half = lb // 2
    across = top * width

    def tall(q, first_row):
        return jnp.concatenate([out[q, first_row], out[q, first_row + 1]], axis=1)

    def gram_part(phase, where, start, count, *accs):
        one, two = accs[:2], accs[2:]

        @pl.loop(0, count // 8)
        def _(c):
            for m in range(2):
                row = start + c * 8 + 4 * m
                pltpu.matmul_push_rhs(
                    jnp.concatenate([tall(where * top + q, row + r)
                                     for r in (0, 2) for q in range(top)], axis=0),
                    0, m, transpose=True)
                pltpu.matmul_acc_lhs(one[m], tall(mc, row), load_staged_rhs=0)
                pltpu.matmul_acc_lhs(two[m], tall(mc, row + 2))

        sums = [pltpu.matmul_pop(one[m])[:, :across] + pltpu.matmul_pop(two[m])[:, across:]
                for m in range(2)]
        gp[phase] = sums[0] + sums[1]

    def grams(phase, *where):
        pl.run_scoped(functools.partial(gram_part, phase, *where),
                      *[pltpu.ACC(m)((width, 2 * across), f32) for _ in range(2) for m in range(2)])

    def part_to(phase, d):
        to = lax.rem(me + d, rows)
        lo = pl.multiple_of(to * rps, rps)
        return to, pltpu.make_async_remote_copy(
            src_ref=gp.at[phase, pl.ds(lo, rps)], dst_ref=rb.at[phase, d],
            send_sem=pss.at[phase, d], recv_sem=prs.at[phase, d], device_id=(to, mc),
            device_id_type=pl.DeviceIdType.MESH)

    def part_in(phase, d):
        return pltpu.make_async_remote_copy(
            src_ref=gp.at[phase, pl.ds(0, rps)], dst_ref=rb.at[phase, d],
            send_sem=pss.at[phase, d], recv_sem=prs.at[phase, d],
            device_id=(lax.rem(me + 1, rows), mc), device_id_type=pl.DeviceIdType.MESH)

    def only(cond, run):
        if reducers == rows:
            run()
        else:
            pl.when(cond)(run)

    def scatter(phase):
        @pl.loop(1, rows)
        def _(d):
            to, c = part_to(phase, d)
            only(to < reducers, lambda: c.start())

    def spot(phase, sender):
        part = lax.rem(sender, parts)
        block = part // top if phase == 0 else 1 - part // top
        lo = pl.multiple_of((part * reducers + sender // parts) * rps, rps)
        return pl.ds(lo, rps), pl.ds(pl.multiple_of(block * across, across), across)

    def all_to(phase, e, sender):
        to = lax.rem(linear + e, everyone)
        return pltpu.make_async_remote_copy(
            src_ref=gs.at[phase], dst_ref=gram.at[spot(phase, sender)], send_sem=ass.at[phase, e],
            recv_sem=ars.at[phase, e], device_id=(to // parts, lax.rem(to, parts)),
            device_id_type=pl.DeviceIdType.MESH)

    def reduce(phase):
        lo = pl.multiple_of(me * rps, rps)
        total = gp[phase, pl.ds(lo, rps)]
        for d in range(1, rows):
            part_in(phase, d).wait_recv()
            total = total + rb[phase, d]
        gs[phase] = total
        gram[spot(phase, linear)] = total

        @pl.loop(1, everyone)
        def _(e):
            all_to(phase, e, linear).start()

    def gathered(phase):
        @pl.loop(1, everyone)
        def _(e):
            sender = lax.rem(linear - e + everyone, everyone)
            only(sender // parts < reducers, lambda: all_to(phase, e, sender).wait_recv())

    arrive(0, chunks, near)
    grams(0, side, 0, lb)
    scatter(0)
    relay(0, chunks // 2)
    arrive(0, chunks // 2, other)
    grams(1, 1 - side, side * half, half)
    scatter(1)
    only(me < reducers, functools.partial(reduce, 0))
    only(me < reducers, functools.partial(reduce, 1))
    relay(chunks // 2, chunks)
    gathered(0)
    eliminate([gram[8 * t:8 * t + 8, :across] for t in range(across // 8)], first_up, first_low)
    arrive(chunks // 2, chunks, other)
    keep_all = pltpu.make_async_copy(out, stored, osem)
    keep_all.start()
    gathered(1)
    for h in halves:
        @pl.loop(0, chunks)
        def _(c):
            for n in range(len(hops)):
                spread(n, h, c).wait_send()

    for phase in range(2):
        @pl.loop(1, rows)
        def _(d):
            to, c = part_to(phase, d)
            only(to < reducers, lambda: c.wait_send())

        @pl.loop(1, everyone)
        def _(e):
            only(me < reducers, lambda: all_to(phase, e, linear).wait_send())

    keep_all.wait()


def filtered(subspace, onsite, blocks, cols):
    rows, parts = lax.axis_size("row"), lax.axis_size("col")
    everyone, hops = rows * parts, len(hops_of(parts))
    width = subspace.shape[0]
    sc, lb, bs, _ = blocks.shape
    groups = len(shifts_of(rows))
    assert lb in (8, 16, 32) and sc >= 8
    ext = pl.next_power_of_2(lb + groups * HALO)
    vm, dma = pltpu.VMEM, pltpu.SemaphoreType.DMA
    full, hw = parts * width, width // HALVES
    half = full // 2
    rps = slice_of(width, rows)
    return pl.pallas_call(
        functools.partial(filter_kernel, rows, parts, lb, sc),
        out_shape=(jax.ShapeDtypeStruct((parts * HALVES, lb, hw, bs), bf16),
                   jax.ShapeDtypeStruct((full, full), f32)) + (jax.ShapeDtypeStruct((half, half), f32),) * 2,
        in_specs=[pl.BlockSpec(memory_space=pl.ANY)] * 4,
        out_specs=[pl.BlockSpec(memory_space=pl.ANY)] + [pl.BlockSpec(memory_space=vm)] * 3,
        scratch_shapes=[vm((sc, lb, bs, bs), bf16)]
        + [vm((ext, hw, bs), bf16)] * (FILTER * HALVES)
        + [vm((groups * HALO, hw, bs), bf16)] * (FILTER * HALVES)
        + [vm((lb, hw, bs), f32)] * ((FILTER - 1) * HALVES)
        + [vm((lb, hw, bs), bf16)] * HALVES
        + [vm((parts * HALVES, lb, hw, bs), bf16), vm((lb, 1, bs), f32), vm(cols.shape[::-1], jnp.int32),
           vm((8, 128), jnp.int32), vm((24 + 2 * sc, 128), jnp.int32),
           pltpu.SMEM((8, 128), jnp.int32), pltpu.SMEM((24 + 2 * sc, 128), jnp.int32)]
        + [vm((2, width, half), f32), vm((2, rps, half), f32), vm((2, rows, rps, half), f32)]
        + [dma((lb // UNROLL,)), dma((HALVES, lb)), dma((HALVES, lb)),
           dma((FILTER, HALVES, groups)), dma((FILTER, HALVES, groups)),
           dma((hops, HALVES, lb // UNROLL)), dma((hops, HALVES, lb // UNROLL)),
           dma((2, rows)), dma((2, rows)), dma((2, everyone)), dma((2, everyone)), dma((4,)), dma],
        compiler_params=pltpu.CompilerParams(
            collective_id=0, has_side_effects=True, vmem_limit_bytes=56 * 1024 * 1024),
        name="filter",
    )(cols.T, subspace, onsite.reshape(lb, 1, bs), blocks)


def eliminate(a, up, low):
    tiles = len(a)
    n = 8 * tiles
    sub = lax.broadcasted_iota(jnp.int32, (8, n), 0)
    lane = lax.broadcasted_iota(jnp.int32, (8, n), 1)
    b = [jnp.where(lane == sub + 8 * t, 1.0, 0.0).astype(f32) for t in range(tiles)]

    def row(v, q):
        return jnp.broadcast_to(v[q:q + 1, :], (8, n))

    for p in range(tiles):
        cols = {t: [jnp.broadcast_to(a[t][:, 8 * p + q:8 * p + q + 1], (8, n)) for q in range(8)]
                for t in range(p, tiles)}
        pivots = jnp.ones((8, n), f32)
        for q in range(8):
            pivot = row(cols[p][q], q)
            pivots = jnp.where(sub == q, pivot, pivots)
            inverse = 1.0 / pivot
            right = [row(cols[p][k], q) for k in range(8)]
            arow, brow = row(a[p], q), row(b[p], q)
            for t in range(p, tiles):
                m = cols[t][q] * inverse
                if t == p:
                    m = jnp.where(sub > q, m, 0.0)
                for k in range(q + 1, 8):
                    cols[t][k] = cols[t][k] - m * right[k]
                a[t] = a[t] - m * arow
                b[t] = b[t] - m * brow
        scale = lax.rsqrt(pivots)
        up[8 * p:8 * p + 8, :] = jnp.where(lane >= sub + 8 * p, a[p] * scale, 0.0)
        low[8 * p:8 * p + 8, :] = b[p] * scale


def finish_kernel(root, col, stored, gram, first_up, first_low, basis, factor, up, low, inv, whole, sem):
    fetch = pltpu.make_async_copy(stored, whole, sem)
    fetch.start()
    parts, lb, _, bs = whole.shape
    width = basis.shape[0]
    full = gram.shape[0]
    half = full // 2
    exact = functools.partial(lax.dot_general, precision=lax.Precision.HIGHEST,
                              preferred_element_type=f32)
    nn, tn = (((1,), (0,)), ((), ())), (((0,), (0,)), ((), ()))
    corner = gram[:half, half:] + gram[half:, :half].T
    across = exact(first_low[...], corner, nn)
    rest = gram[half:, half:] - exact(across, across, tn)
    eliminate([rest[8 * t:8 * t + 8, :] for t in range(half // 8)], up, low)
    factor[half:, :half] = jnp.zeros((half, half), f32)
    inv[:half, half:] = jnp.zeros((half, half), f32)
    inv[:half, :half] = first_low[...]
    inv[half:, half:] = low[...]
    inv[half:, :half] = -exact(low[...], exact(across, first_low[...], tn), nn)
    factor[:half, :half] = first_up[...] * (1.0 / root)
    factor[:half, half:] = across * (1.0 / root)
    factor[half:, half:] = up[...] * (1.0 / root)

    mine = inv[pl.ds(pl.multiple_of(col[0] * width, width), width), :] * root
    high = mine.astype(bf16)
    rest = mine - high.astype(f32)
    mid = rest.astype(bf16)
    last = (rest - mid.astype(f32)).astype(bf16)
    left = jnp.concatenate([high, mid, last], axis=0)

    fetch.wait()
    for k in range(lb):
        right = jnp.concatenate([whole[q, k] for q in range(parts)], axis=0)
        r = jnp.dot(left, right, preferred_element_type=f32)
        basis[:, k * bs:(k + 1) * bs] = r[:width] + (r[width:2 * width] + r[2 * width:])


def body(subspace, onsite, blocks, cols):
    row_count = lax.axis_size("row")
    part_width, local_rows = subspace.shape
    whole, gram, first_up, first_low = filtered(subspace, onsite, blocks, cols)
    full = gram.shape[0]
    half = full // 2
    root = math.sqrt(row_count * local_rows)
    vm = pltpu.VMEM
    return pl.pallas_call(
        functools.partial(finish_kernel, root),
        out_shape=(jax.ShapeDtypeStruct((part_width, local_rows), f32),
                   jax.ShapeDtypeStruct((full, full), f32)),
        in_specs=[pl.BlockSpec(memory_space=pltpu.SMEM), pl.BlockSpec(memory_space=pltpu.HBM),
                  *[pl.BlockSpec(memory_space=vm)] * 3],
        out_specs=[pl.BlockSpec(memory_space=vm)] * 2,
        scratch_shapes=[vm((half, half), f32), vm((half, half), f32), vm((full, full), f32), vm(whole.shape, bf16), pltpu.SemaphoreType.DMA],
        compiler_params=pltpu.CompilerParams(vmem_limit_bytes=60 * 1024 * 1024),
        name="finish",
    )(lax.axis_index("col").astype(jnp.int32).reshape(1), whole, gram, first_up, first_low)


def solution(mesh):
    in_specs = (P("col", "row"), P("row"), P(None, "row", None, None), P())
    out_specs = (P("col", "row"), P())
    return jax.shard_map(body, mesh=mesh, in_specs=in_specs, out_specs=out_specs, check_vma=False)
```

```python
import functools
import math

import jax
import jax.numpy as jnp
from jax import lax
from jax.experimental import pallas as pl
from jax.experimental.pallas import tpu as pltpu
from jax.sharding import PartitionSpec as P

HALO = 4
FILTER = 4
UNROLL = 4
HALVES = 1
filter_scale = 0.4
f32 = jnp.float32
bf16 = jnp.bfloat16


def shifts_of(rows):
    return (rows // 2, 2, 1, -1)


def bits_below(k):
    return lax.shift_left(jnp.ones_like(k), k) - 1


def ones_in(x):
    return lax.population_count(x)


def folded(x, axis):
    step = x.shape[axis] // 2
    while step:
        x = x | pltpu.roll(x, step, axis)
        step //= 2
    return x


def tiles_of(sc):
    return list(range(0, sc - 7, 8)) + ([sc - 8] if sc % 8 else [])


def masks_of(cvm, rows, me, lb, sc):
    shifts = shifts_of(rows)
    groups = len(shifts)
    lane = lax.broadcasted_iota(jnp.int32, (8, 128), 1)
    sub = lax.broadcasted_iota(jnp.int32, (8, 128), 0)
    per = 128 // lb

    def picked(device, owners):
        start = pl.multiple_of(device // per * 128, 128)
        live = lane // lb == lax.rem(device, per)
        found = [jnp.zeros((8, 128), jnp.int32) for _ in owners]
        for o in tiles_of(sc):
            v = cvm[o:o + 8, pl.ds(start, 128)]
            for n, owner in enumerate(owners):
                rel = v - owner * lb
                hit = live & (rel >= 0) & (rel < lb)
                found[n] = found[n] | jnp.where(
                    hit, lax.shift_left(jnp.ones_like(rel), rel & (lb - 1)), 0)
        return found

    found = picked(me, [lax.rem(me + d + rows, rows) for d in shifts])
    for d in shifts:
        found += picked(lax.rem(me - d + rows, rows), [me])
    both = jnp.zeros((8, 128), jnp.int32)
    for n, x in enumerate(found):
        both = jnp.where(sub == n, folded(x, 0), both)
    assert groups == 4
    return folded(both, 1)


def mask_row(masks, n):
    return jnp.broadcast_to(masks[n:n + 1, :], (8, 128))


def byte_of(word, n, limit):
    return lax.shift_right_logical(word, 8 * n) & (limit - 1)


def packed_exports(masks, lb, names):
    k = lax.broadcasted_iota(jnp.int32, (8, 128), 1)
    low = jnp.minimum(k, lb - 1)
    hit = (k < lb) & ((lax.shift_right_logical(masks, low) & 1) == 1)
    rank = ones_in(masks & bits_below(low))
    word = jnp.zeros((8, 128), jnp.int32)
    for m in range(HALO):
        word = word | jnp.where(hit & (rank == m), lax.shift_left(names, jnp.full_like(names, 8 * m)), 0)
    return folded(word, 1)


def order_of(masks, groups, at):
    taken = jnp.zeros((8, 128), jnp.int32)
    base = jnp.zeros((8, 128), jnp.int32)
    place = jnp.zeros((8, 128), jnp.int32)
    below = bits_below(at)
    for g in range(groups + 1):
        left = ~taken
        mine = left if g == groups else mask_row(masks, groups + g) & left
        here = (lax.shift_right_logical(mine, at) & 1) == 1
        place = jnp.where(here, base + ones_in(mine & below), place)
        base = base + ones_in(mine)
        taken = taken | mine
    return place


def flip(c, bit):
    return c + bit - 2 * bit * lax.rem(c // bit, 2)


def hops_of(parts):
    hops, held, bit = [], [0], parts // 2
    while bit:
        hops += [(bit, m) for m in held]
        held += [m + bit for m in held]
        bit //= 2
    return hops


def slice_of(width, rows):
    return max(8, width // rows)


def filter_kernel(rows, parts, lb, sc, cols, sub, ons_in, blk, stored, gram, first_up,
                  first_low, bm, *refs):
    refs = list(refs)
    take = lambda n: [refs.pop(0) for _ in range(n)]
    halves = range(HALVES)
    xs = [take(HALVES) for _ in range(FILTER)]
    snds = [take(HALVES) for _ in range(FILTER)]
    ys = [take(HALVES) for _ in range(FILTER - 1)]
    s0 = take(HALVES)
    (out, ons, cvm, early_v, late_v, early, late, gp, gs, rb, bsem, xsem, csem, ssem, rsem,
     wss, wrs, pss, prs, ass, ars, tsem, osem) = refs
    me = lax.axis_index("row")
    mc = lax.axis_index("col")
    everyone = rows * parts
    linear = me * parts + mc
    width = sub.shape[0]
    hw = width // HALVES
    hops = hops_of(parts)
    rps = slice_of(width, rows)
    reducers = width // rps
    shifts = shifts_of(rows)
    groups = len(shifts)
    bs = blk.shape[-1]
    chunks = lb // UNROLL

    def load(c):
        part = pl.ds(c * UNROLL, UNROLL)
        return pltpu.make_async_copy(blk.at[:, part], bm.at[:, part], bsem.at[c])

    def first(i, h):
        cut = sub.at[pl.ds(h * hw, hw), pl.ds(pl.multiple_of(i * bs, bs), bs)]
        return (pltpu.make_async_copy(cut, xs[0][h].at[i], xsem.at[h, i]),
                pltpu.make_async_copy(cut, s0[h].at[i], csem.at[h, i]))

    named = pltpu.make_async_copy(cols, cvm, tsem.at[0])
    named.start()
    barrier = pltpu.get_barrier_semaphore()

    @pl.loop(1, everyone)
    def _(e):
        to = lax.rem(linear + e, everyone)
        pl.semaphore_signal(barrier, inc=1, device_id=(to // parts, lax.rem(to, parts)),
                            device_id_type=pl.DeviceIdType.MESH)

    for h in halves:
        @pl.loop(0, lb)
        def _(i):
            first(i, h)[1].start()

    energies = pltpu.make_async_copy(ons_in, ons, tsem.at[1])
    energies.start()

    @pl.loop(0, chunks)
    def _(c):
        load(c).start()

    named.wait()
    masks = masks_of(cvm, rows, me, lb, sc)
    lane = lax.broadcasted_iota(jnp.int32, (8, 128), 1)
    sublane = lax.broadcasted_iota(jnp.int32, (8, 128), 0)
    early_v[...] = packed_exports(masks, lb, lane)
    to_early = pltpu.make_async_copy(early_v, early, tsem.at[2])
    to_early.start()

    to_late = pltpu.make_async_copy(late_v, late, tsem.at[3])
    shift = lax.rem(me, 128 // lb) * lb
    pn, pp, span = 24, 24 + sc, xs[0][0].shape[0]

    def export(k, g, m):
        return byte_of(early[groups + g, 0] if k == 0 else late[groups + g, 0], m, lb)

    def permuted(j):
        return byte_of(late[8 + lax.rem(j, 8), 0], j // 8, lb)

    def offset_of(g):
        if isinstance(g, int):
            return shifts[g]
        found = shifts[-1]
        for n in range(groups - 1):
            found = jnp.where(g == n, shifts[n], found)
        return found

    def copy(k, h, g):
        return pltpu.make_async_remote_copy(
            src_ref=snds[k][h].at[pl.ds(g * HALO, HALO)],
            dst_ref=xs[k][h].at[pl.ds(lb + g * HALO, HALO)],
            send_sem=ssem.at[k, h, g], recv_sem=rsem.at[k, h, g],
            device_id=(lax.rem(me - offset_of(g) + rows, rows), mc),
            device_id_type=pl.DeviceIdType.MESH)

    def pack(k, h, g, source):
        for m in range(HALO):
            snds[k][h][g * HALO + m] = source[export(k, g, m)].astype(bf16)

    for h in halves:
        @pl.loop(0, lb)
        def _(i):
            first(i, h)[1].wait()

        to_early.wait()
        for g in range(groups):
            pack(0, h, g, s0[h])
        if h == 0:
            pl.semaphore_wait(barrier, everyone - 1)
        for g in range(groups):
            copy(0, h, g).start()

    for h in halves:
        @pl.loop(0, lb)
        def _(i):
            first(i, h)[0].start()

    inverse = order_of(masks, groups, jnp.minimum(lane, lb - 1))
    late_v[0:8, :] = packed_exports(masks, lb, inverse)
    word = jnp.zeros((8, 128), jnp.int32)
    for q in range(lb // 8):
        word = word | jnp.where((lane < lb) & (inverse == 8 * q + sublane),
                                lax.shift_left(lane, jnp.full_like(lane, 8 * q)), 0)
    late_v[8:16, :] = folded(word, 1)
    late_v[16:24, :] = inverse
    per = 128 // lb
    start = pl.multiple_of(me // per * 128, 128)
    for o in tiles_of(sc):
        v = cvm[o:o + 8, pl.ds(start, 128)]
        rel = v - me * lb
        near = (rel >= 0) & (rel < lb)
        low = rel & (lb - 1)
        far = jnp.zeros((8, 128), jnp.int32)
        for g, d in enumerate(shifts):
            there = v - lax.rem(me + d + rows, rows) * lb
            at = there & (lb - 1)
            far = jnp.where((there >= 0) & (there < lb),
                            lb + HALO * g + ones_in(mask_row(masks, g) & bits_below(at)), far)
        late_v[24 + o:32 + o, :] = jnp.where(near, low, far)
        late_v[24 + sc + o:32 + sc + o, :] = jnp.where(near, order_of(masks, groups, low), far)
    to_late.start()
    for h in halves:
        @pl.loop(0, lb)
        def _(i):
            first(i, h)[0].wait()

    energies.wait()
    to_late.wait()

    def place(k, j):
        i = j if k == FILTER - 1 else permuted(j)
        own = late[16, j] & (lb - 1) if k == FILTER - 1 else (i if k == 0 else j)
        return i, own

    def feed(k, first_row, accs):
        base = pn if k == 0 else pp
        x = xs[k][0]
        at = [place(k, first_row + u)[0] for u in range(UNROLL)]
        for t in range(sc // 2):
            for m in range(2):
                pair = at[2 * m:2 * m + 2]
                pltpu.matmul_push_rhs(jnp.concatenate(
                    [jnp.concatenate([bm[2 * t, i], bm[2 * t + 1, i]], axis=0) for i in pair],
                    axis=1), t % 2, m)
                for u, i in enumerate(pair):
                    left = jnp.concatenate(
                        [x[late[base + 2 * t + s, shift + i] & (span - 1)] for s in range(2)], axis=1)
                    pltpu.matmul_acc_lhs(accs[m][u], left,
                                         load_staged_rhs=t % 2 if u == 0 else None)

    def settle(k, row, acc, u):
        i, own = place(k, row)
        total = pltpu.matmul_pop(acc)[:, u * bs:(u + 1) * bs]
        total = total + ons[i] * xs[k][0][own].astype(f32)
        if k == 0:
            return filter_scale * total
        prev = xs[0][0][i].astype(f32) if k == 1 else ys[k - 2][0][own]
        return 2.0 * filter_scale * total - prev

    def turn(piece, c):
        return lax.rem(c + (1 - piece // (parts // 2)) * (chunks // 2), chunks)

    def spread(n, h, c):
        bit, m = hops[n]
        piece = mc
        for b in (m & (1 << t) for t in range(m.bit_length())):
            if b:
                piece = flip(piece, b)
        part = out.at[piece * HALVES + h, pl.ds(turn(piece, c) * UNROLL, UNROLL)]
        return pltpu.make_async_remote_copy(
            src_ref=part, dst_ref=part, send_sem=wss.at[n, h, c], recv_sem=wrs.at[n, h, c],
            device_id=(me, flip(mc, bit)), device_id_type=pl.DeviceIdType.MESH)

    firsts = [n for n, (_, m) in enumerate(hops) if m == 0]

    @pl.loop(0, chunks)
    def _(c):
        load(c).wait()

    def keep(k, j, value):
        low = value.astype(bf16)
        if k < FILTER - 1:
            xs[k + 1][0][j] = low
            ys[k][0][j] = value
        else:
            out[mc, j] = low

    def rows_of(k, c):
        return (turn(mc, c) if k == FILTER - 1 else c) * UNROLL

    def chunk(k, c, accs):
        for m in range(2):
            for u in range(2):
                j = rows_of(k, c) + 2 * m + u
                keep(k, j, settle(k, j, accs[m][u], u))

    def filtering(*flat):
        sets = [[flat[4 * q + 2 * m:4 * q + 2 * m + 2] for m in range(2)] for q in range(2)]
        for k in range(FILTER):
            for g in range(groups):
                copy(k, 0, g).wait_recv()
            last = k == FILTER - 1

            def sent(c):
                if last:
                    for n in firsts:
                        spread(n, 0, c).start()

            @pl.loop(0, groups)
            def _(c):
                feed(k, rows_of(k, c), sets[0])
                chunk(k, c, sets[0])
                if not last:
                    pack(k + 1, 0, c, ys[k][0])
                    copy(k + 1, 0, c).start()
                sent(c)

            @pl.loop(groups // 2, chunks // 2)
            def _(cc):
                for q in range(2):
                    feed(k, rows_of(k, 2 * cc + q), sets[q])
                for q in range(2):
                    chunk(k, 2 * cc + q, sets[q])
                for q in range(2):
                    sent(2 * cc + q)

    pl.run_scoped(filtering, *[pltpu.ACC(m)((width, 2 * bs), f32)
                               for _ in range(2) for m in range(2) for _ in range(2)])

    for k in range(FILTER):
        for h in halves:
            for g in range(groups):
                copy(k, h, g).wait_send()

    needs = {n: max(q for q in range(n) if sum(hops[q]) == m)
             for n, (_, m) in enumerate(hops) if m}
    def relay(lo, hi):
        for h in halves:
            @pl.loop(lo, hi)
            def _(c):
                got = set()
                for n in needs:
                    if needs[n] not in got:
                        spread(needs[n], h, c).wait_recv()
                        got.add(needs[n])
                    spread(n, h, c).start()

    def arrive(lo, hi, picked):
        for h in halves:
            @pl.loop(lo, hi)
            def _(c):
                for n in picked:
                    spread(n, h, c).wait_recv()

    top = parts // 2
    leaves = [n for n in range(len(hops)) if n not in needs.values()]
    near = [n for n in leaves if sum(hops[n]) < top]
    other = [n for n in leaves if sum(hops[n]) >= top]
    side = mc // top
    half = lb // 2
    across = top * width

    def tall(q, first_row):
        return jnp.concatenate([out[q, first_row], out[q, first_row + 1]], axis=1)

    def gram_part(phase, where, start, count, *accs):
        one, two = accs[:2], accs[2:]

        @pl.loop(0, count // 8)
        def _(c):
            for m in range(2):
                row = start + c * 8 + 4 * m
                pltpu.matmul_push_rhs(
                    jnp.concatenate([tall(where * top + q, row + r)
                                     for r in (0, 2) for q in range(top)], axis=0),
                    0, m, transpose=True)
                pltpu.matmul_acc_lhs(one[m], tall(mc, row), load_staged_rhs=0)
                pltpu.matmul_acc_lhs(two[m], tall(mc, row + 2))

        sums = [pltpu.matmul_pop(one[m])[:, :across] + pltpu.matmul_pop(two[m])[:, across:]
                for m in range(2)]
        gp[phase] = sums[0] + sums[1]

    def grams(phase, *where):
        pl.run_scoped(functools.partial(gram_part, phase, *where),
                      *[pltpu.ACC(m)((width, 2 * across), f32) for _ in range(2) for m in range(2)])

    def part_to(phase, d):
        to = lax.rem(me + d, rows)
        lo = pl.multiple_of(to * rps, rps)
        return to, pltpu.make_async_remote_copy(
            src_ref=gp.at[phase, pl.ds(lo, rps)], dst_ref=rb.at[phase, d],
            send_sem=pss.at[phase, d], recv_sem=prs.at[phase, d], device_id=(to, mc),
            device_id_type=pl.DeviceIdType.MESH)

    def part_in(phase, d):
        return pltpu.make_async_remote_copy(
            src_ref=gp.at[phase, pl.ds(0, rps)], dst_ref=rb.at[phase, d],
            send_sem=pss.at[phase, d], recv_sem=prs.at[phase, d],
            device_id=(lax.rem(me + 1, rows), mc), device_id_type=pl.DeviceIdType.MESH)

    def only(cond, run):
        if reducers == rows:
            run()
        else:
            pl.when(cond)(run)

    def scatter(phase):
        @pl.loop(1, rows)
        def _(d):
            to, c = part_to(phase, d)
            only(to < reducers, lambda: c.start())

    def spot(phase, sender):
        part = lax.rem(sender, parts)
        block = part // top if phase == 0 else 1 - part // top
        lo = pl.multiple_of((part * reducers + sender // parts) * rps, rps)
        return pl.ds(lo, rps), pl.ds(pl.multiple_of(block * across, across), across)

    def all_to(phase, e, sender):
        to = lax.rem(linear + e, everyone)
        return pltpu.make_async_remote_copy(
            src_ref=gs.at[phase], dst_ref=gram.at[spot(phase, sender)], send_sem=ass.at[phase, e],
            recv_sem=ars.at[phase, e], device_id=(to // parts, lax.rem(to, parts)),
            device_id_type=pl.DeviceIdType.MESH)

    def reduce(phase):
        lo = pl.multiple_of(me * rps, rps)
        total = gp[phase, pl.ds(lo, rps)]
        for d in range(1, rows):
            part_in(phase, d).wait_recv()
            total = total + rb[phase, d]
        gs[phase] = total
        gram[spot(phase, linear)] = total

        @pl.loop(1, everyone)
        def _(e):
            all_to(phase, e, linear).start()

    def gathered(phase):
        @pl.loop(1, everyone)
        def _(e):
            sender = lax.rem(linear - e + everyone, everyone)
            only(sender // parts < reducers, lambda: all_to(phase, e, sender).wait_recv())

    arrive(0, chunks, near)
    grams(0, side, 0, lb)
    scatter(0)
    relay(0, chunks // 2)
    arrive(0, chunks // 2, other)
    grams(1, 1 - side, side * half, half)
    scatter(1)
    only(me < reducers, functools.partial(reduce, 0))
    only(me < reducers, functools.partial(reduce, 1))
    relay(chunks // 2, chunks)
    gathered(0)
    arrive(chunks // 2, chunks, other)
    keep_all = pltpu.make_async_copy(out, stored, osem)
    keep_all.start()
    eliminate([gram[8 * t:8 * t + 8, :across] for t in range(across // 8)], first_up, first_low)
    gathered(1)
    for h in halves:
        @pl.loop(0, chunks)
        def _(c):
            for n in range(len(hops)):
                spread(n, h, c).wait_send()

    for phase in range(2):
        @pl.loop(1, rows)
        def _(d):
            to, c = part_to(phase, d)
            only(to < reducers, lambda: c.wait_send())

        @pl.loop(1, everyone)
        def _(e):
            only(me < reducers, lambda: all_to(phase, e, linear).wait_send())

    keep_all.wait()


def filtered(subspace, onsite, blocks, cols):
    rows, parts = lax.axis_size("row"), lax.axis_size("col")
    everyone, hops = rows * parts, len(hops_of(parts))
    width = subspace.shape[0]
    sc, lb, bs, _ = blocks.shape
    groups = len(shifts_of(rows))
    assert lb in (8, 16, 32) and sc >= 8
    ext = pl.next_power_of_2(lb + groups * HALO)
    vm, dma = pltpu.VMEM, pltpu.SemaphoreType.DMA
    full, hw = parts * width, width // HALVES
    half = full // 2
    rps = slice_of(width, rows)
    return pl.pallas_call(
        functools.partial(filter_kernel, rows, parts, lb, sc),
        out_shape=(jax.ShapeDtypeStruct((parts * HALVES, lb, hw, bs), bf16),
                   jax.ShapeDtypeStruct((full, full), f32)) + (jax.ShapeDtypeStruct((half, half), f32),) * 2,
        in_specs=[pl.BlockSpec(memory_space=pl.ANY)] * 4,
        out_specs=[pl.BlockSpec(memory_space=pl.ANY)] + [pl.BlockSpec(memory_space=vm)] * 3,
        scratch_shapes=[vm((sc, lb, bs, bs), bf16)]
        + [vm((ext, hw, bs), bf16)] * (FILTER * HALVES)
        + [vm((groups * HALO, hw, bs), bf16)] * (FILTER * HALVES)
        + [vm((lb, hw, bs), f32)] * ((FILTER - 1) * HALVES)
        + [vm((lb, hw, bs), bf16)] * HALVES
        + [vm((parts * HALVES, lb, hw, bs), bf16), vm((lb, 1, bs), f32), vm(cols.shape[::-1], jnp.int32),
           vm((8, 128), jnp.int32), vm((24 + 2 * sc, 128), jnp.int32),
           pltpu.SMEM((8, 128), jnp.int32), pltpu.SMEM((24 + 2 * sc, 128), jnp.int32)]
        + [vm((2, width, half), f32), vm((2, rps, half), f32), vm((2, rows, rps, half), f32)]
        + [dma((lb // UNROLL,)), dma((HALVES, lb)), dma((HALVES, lb)),
           dma((FILTER, HALVES, groups)), dma((FILTER, HALVES, groups)),
           dma((hops, HALVES, lb // UNROLL)), dma((hops, HALVES, lb // UNROLL)),
           dma((2, rows)), dma((2, rows)), dma((2, everyone)), dma((2, everyone)), dma((4,)), dma],
        compiler_params=pltpu.CompilerParams(
            collective_id=0, has_side_effects=True, vmem_limit_bytes=56 * 1024 * 1024),
        name="filter",
    )(cols.T, subspace, onsite.reshape(lb, 1, bs), blocks)


def eliminate(a, up, low):
    tiles = len(a)
    n = 8 * tiles
    sub = lax.broadcasted_iota(jnp.int32, (8, n), 0)
    lane = lax.broadcasted_iota(jnp.int32, (8, n), 1)
    b = [jnp.where(lane == sub + 8 * t, 1.0, 0.0).astype(f32) for t in range(tiles)]

    def row(v, q):
        return jnp.broadcast_to(v[q:q + 1, :], (8, n))

    for p in range(tiles):
        cols = {t: [jnp.broadcast_to(a[t][:, 8 * p + q:8 * p + q + 1], (8, n)) for q in range(8)]
                for t in range(p, tiles)}
        pivots = jnp.ones((8, n), f32)
        for q in range(8):
            pivot = row(cols[p][q], q)
            pivots = jnp.where(sub == q, pivot, pivots)
            inverse = 1.0 / pivot
            right = [row(cols[p][k], q) for k in range(8)]
            arow, brow = row(a[p], q), row(b[p], q)
            for t in range(p, tiles):
                m = cols[t][q] * inverse
                if t == p:
                    m = jnp.where(sub > q, m, 0.0)
                for k in range(q + 1, 8):
                    cols[t][k] = cols[t][k] - m * right[k]
                a[t] = a[t] - m * arow
                b[t] = b[t] - m * brow
        scale = lax.rsqrt(pivots)
        up[8 * p:8 * p + 8, :] = jnp.where(lane >= sub + 8 * p, a[p] * scale, 0.0)
        low[8 * p:8 * p + 8, :] = b[p] * scale


def finish_kernel(root, col, stored, gram_in, up_in, low_in, basis_out, factor_out,
                  basis, factor, up, low, inv, gram, first_up, first_low, whole, sem):
    operands = [pltpu.make_async_copy(*pair, sem.at[6 + n]) for n, pair in enumerate(
        ((low_in, first_low), (gram_in, gram), (up_in, first_up)))]
    for operand in operands:
        operand.start()
    fetch = pltpu.make_async_copy(stored, whole, sem.at[0])
    fetch.start()
    parts, lb, _, bs = whole.shape
    width = basis.shape[0]
    full = gram.shape[0]
    half = full // 2
    exact = functools.partial(lax.dot_general, precision=lax.Precision.HIGHEST,
                              preferred_element_type=f32)
    nn, tn = (((1,), (0,)), ((), ())), (((0,), (0,)), ((), ()))
    operands[0].wait()
    operands[1].wait()
    corner = gram[:half, half:] + gram[half:, :half].T
    across = exact(first_low[...], corner, nn)
    rest = gram[half:, half:] - exact(across, across, tn)
    eliminate([rest[8 * t:8 * t + 8, :] for t in range(half // 8)], up, low)
    factor[half:, :half] = jnp.zeros((half, half), f32)
    inv[:half, half:] = jnp.zeros((half, half), f32)
    inv[:half, :half] = first_low[...]
    inv[half:, half:] = low[...]
    inv[half:, :half] = -exact(low[...], exact(across, first_low[...], tn), nn)
    operands[2].wait()
    factor[:half, :half] = first_up[...] * (1.0 / root)
    factor[:half, half:] = across * (1.0 / root)
    factor[half:, half:] = up[...] * (1.0 / root)
    put = [pltpu.make_async_copy(factor, factor_out, sem.at[1])]
    put[0].start()

    mine = inv[pl.ds(pl.multiple_of(col[0] * width, width), width), :] * root
    high = mine.astype(bf16)
    rest = mine - high.astype(f32)
    mid = rest.astype(bf16)
    last = (rest - mid.astype(f32)).astype(bf16)
    left = jnp.concatenate([high, mid, last], axis=0)

    fetch.wait()
    every = lb // 4
    for k in range(lb):
        right = jnp.concatenate([whole[q, k] for q in range(parts)], axis=0)
        r = jnp.dot(left, right, preferred_element_type=f32)
        basis[:, k * bs:(k + 1) * bs] = r[:width] + (r[width:2 * width] + r[2 * width:])
        if k % every == every - 1:
            cut = pl.ds((k + 1 - every) * bs, every * bs)
            put.append(pltpu.make_async_copy(basis.at[:, cut], basis_out.at[:, cut],
                                             sem.at[2 + k // every]))
            put[-1].start()
    for copy in put:
        copy.wait()


def body(subspace, onsite, blocks, cols):
    row_count = lax.axis_size("row")
    part_width, local_rows = subspace.shape
    whole, gram, first_up, first_low = filtered(subspace, onsite, blocks, cols)
    full = gram.shape[0]
    half = full // 2
    root = math.sqrt(row_count * local_rows)
    vm = pltpu.VMEM
    return pl.pallas_call(
        functools.partial(finish_kernel, root),
        out_shape=(jax.ShapeDtypeStruct((part_width, local_rows), f32),
                   jax.ShapeDtypeStruct((full, full), f32)),
        in_specs=[pl.BlockSpec(memory_space=pltpu.SMEM), *[pl.BlockSpec(memory_space=pltpu.HBM)] * 4],
        out_specs=[pl.BlockSpec(memory_space=pl.ANY)] * 2,
        scratch_shapes=[vm((part_width, local_rows), f32), vm((full, full), f32),
                        vm((half, half), f32), vm((half, half), f32), vm((full, full), f32),
                        vm((full, full), f32), vm((half, half), f32), vm((half, half), f32),
                        vm(whole.shape, bf16), pltpu.SemaphoreType.DMA((9,))],
        compiler_params=pltpu.CompilerParams(vmem_limit_bytes=60 * 1024 * 1024),
        name="finish",
    )(lax.axis_index("col").astype(jnp.int32).reshape(1), whole, gram, first_up, first_low)


def solution(mesh):
    in_specs = (P("col", "row"), P("row"), P(None, "row", None, None), P())
    out_specs = (P("col", "row"), P())
    return jax.shard_map(body, mesh=mesh, in_specs=in_specs, out_specs=out_specs, check_vma=False)
```

```python
import functools
import math

import jax
import jax.numpy as jnp
from jax import lax
from jax.experimental import pallas as pl
from jax.experimental.pallas import tpu as pltpu
from jax.sharding import PartitionSpec as P

HALO = 4
FILTER = 4
UNROLL = 4
HALVES = 1
filter_scale = 0.4
f32 = jnp.float32
bf16 = jnp.bfloat16


def shifts_of(rows):
    return (1, -1, 2, rows // 2)


def bits_below(k):
    return lax.shift_left(jnp.ones_like(k), k) - 1


def ones_in(x):
    return lax.population_count(x)


def folded(x, axis):
    step = x.shape[axis] // 2
    while step:
        x = x | pltpu.roll(x, step, axis)
        step //= 2
    return x


def tiles_of(sc):
    return list(range(0, sc - 7, 8)) + ([sc - 8] if sc % 8 else [])


def masks_of(cvm, rows, me, lb, sc):
    shifts = shifts_of(rows)
    groups = len(shifts)
    lane = lax.broadcasted_iota(jnp.int32, (8, 128), 1)
    sub = lax.broadcasted_iota(jnp.int32, (8, 128), 0)
    per = 128 // lb

    def picked(device, owners):
        start = pl.multiple_of(device // per * 128, 128)
        live = lane // lb == lax.rem(device, per)
        found = [jnp.zeros((8, 128), jnp.int32) for _ in owners]
        for o in tiles_of(sc):
            v = cvm[o:o + 8, pl.ds(start, 128)]
            for n, owner in enumerate(owners):
                rel = v - owner * lb
                hit = live & (rel >= 0) & (rel < lb)
                found[n] = found[n] | jnp.where(
                    hit, lax.shift_left(jnp.ones_like(rel), rel & (lb - 1)), 0)
        return found

    found = picked(me, [lax.rem(me + d + rows, rows) for d in shifts])
    for d in shifts:
        found += picked(lax.rem(me - d + rows, rows), [me])
    both = jnp.zeros((8, 128), jnp.int32)
    for n, x in enumerate(found):
        both = jnp.where(sub == n, folded(x, 0), both)
    assert groups == 4
    return folded(both, 1)


def mask_row(masks, n):
    return jnp.broadcast_to(masks[n:n + 1, :], (8, 128))


def byte_of(word, n, limit):
    return lax.shift_right_logical(word, 8 * n) & (limit - 1)


def packed_exports(masks, lb, names):
    k = lax.broadcasted_iota(jnp.int32, (8, 128), 1)
    low = jnp.minimum(k, lb - 1)
    hit = (k < lb) & ((lax.shift_right_logical(masks, low) & 1) == 1)
    rank = ones_in(masks & bits_below(low))
    word = jnp.zeros((8, 128), jnp.int32)
    for m in range(HALO):
        word = word | jnp.where(hit & (rank == m), lax.shift_left(names, jnp.full_like(names, 8 * m)), 0)
    return folded(word, 1)


def order_of(masks, groups, at):
    taken = jnp.zeros((8, 128), jnp.int32)
    base = jnp.zeros((8, 128), jnp.int32)
    place = jnp.zeros((8, 128), jnp.int32)
    below = bits_below(at)
    for g in range(groups + 1):
        left = ~taken
        mine = left if g == groups else mask_row(masks, groups + g) & left
        here = (lax.shift_right_logical(mine, at) & 1) == 1
        place = jnp.where(here, base + ones_in(mine & below), place)
        base = base + ones_in(mine)
        taken = taken | mine
    return place


def flip(c, bit):
    return c + bit - 2 * bit * lax.rem(c // bit, 2)


def hops_of(parts):
    hops, held, bit = [], [0], parts // 2
    while bit:
        hops += [(bit, m) for m in held]
        held += [m + bit for m in held]
        bit //= 2
    return hops


def slice_of(width, rows):
    return max(8, width // rows)


def filter_kernel(rows, parts, lb, sc, cols, sub, ons_in, blk, stored, gram_out, up_out,
                  low_out, bm, *refs):
    refs = list(refs)
    take = lambda n: [refs.pop(0) for _ in range(n)]
    halves = range(HALVES)
    xs = [take(HALVES) for _ in range(FILTER)]
    snds = [take(HALVES) for _ in range(FILTER)]
    ys = [take(HALVES) for _ in range(FILTER - 1)]
    s0 = take(HALVES)
    (out, ons, cvm, early_v, late_v, early, late, gp, gs, rb, bsem, xsem, csem, ssem, rsem,
     wss, wrs, pss, prs, ass, ars, tsem, osem, gram, first_up, first_low) = refs
    me = lax.axis_index("row")
    mc = lax.axis_index("col")
    everyone = rows * parts
    linear = me * parts + mc
    width = sub.shape[0]
    hw = width // HALVES
    hops = hops_of(parts)
    rps = slice_of(width, rows)
    reducers = width // rps
    shifts = shifts_of(rows)
    groups = len(shifts)
    bs = blk.shape[-1]
    chunks = lb // UNROLL

    def load(c):
        part = pl.ds(c * UNROLL, UNROLL)
        return pltpu.make_async_copy(blk.at[:, part], bm.at[:, part], bsem.at[c])

    def first(i, h):
        cut = sub.at[pl.ds(h * hw, hw), pl.ds(pl.multiple_of(i * bs, bs), bs)]
        return (pltpu.make_async_copy(cut, xs[0][h].at[i], xsem.at[h, i]),
                pltpu.make_async_copy(cut, s0[h].at[i], csem.at[h, i]))

    named = pltpu.make_async_copy(cols, cvm, tsem.at[0])
    named.start()
    barrier = pltpu.get_barrier_semaphore()

    @pl.loop(1, everyone)
    def _(e):
        to = lax.rem(linear + e, everyone)
        pl.semaphore_signal(barrier, inc=1, device_id=(to // parts, lax.rem(to, parts)),
                            device_id_type=pl.DeviceIdType.MESH)

    for h in halves:
        @pl.loop(0, lb)
        def _(i):
            first(i, h)[1].start()

    energies = pltpu.make_async_copy(ons_in, ons, tsem.at[1])
    energies.start()

    @pl.loop(0, chunks)
    def _(c):
        load(c).start()

    named.wait()
    masks = masks_of(cvm, rows, me, lb, sc)
    lane = lax.broadcasted_iota(jnp.int32, (8, 128), 1)
    sublane = lax.broadcasted_iota(jnp.int32, (8, 128), 0)
    early_v[...] = packed_exports(masks, lb, lane)
    to_early = pltpu.make_async_copy(early_v, early, tsem.at[2])
    to_early.start()

    to_late = pltpu.make_async_copy(late_v, late, tsem.at[3])
    shift = lax.rem(me, 128 // lb) * lb
    pn, pp, span = 24, 24 + sc, xs[0][0].shape[0]

    def export(k, g, m):
        return byte_of(early[groups + g, 0] if k == 0 else late[groups + g, 0], m, lb)

    def permuted(j):
        return byte_of(late[8 + lax.rem(j, 8), 0], j // 8, lb)

    def offset_of(g):
        if isinstance(g, int):
            return shifts[g]
        found = shifts[-1]
        for n in range(groups - 1):
            found = jnp.where(g == n, shifts[n], found)
        return found

    def copy(k, h, g):
        return pltpu.make_async_remote_copy(
            src_ref=snds[k][h].at[pl.ds(g * HALO, HALO)],
            dst_ref=xs[k][h].at[pl.ds(lb + g * HALO, HALO)],
            send_sem=ssem.at[k, h, g], recv_sem=rsem.at[k, h, g],
            device_id=(lax.rem(me - offset_of(g) + rows, rows), mc),
            device_id_type=pl.DeviceIdType.MESH)

    def pack(k, h, g, source):
        for m in range(HALO):
            snds[k][h][g * HALO + m] = source[export(k, g, m)].astype(bf16)

    for h in halves:
        @pl.loop(0, lb)
        def _(i):
            first(i, h)[1].wait()

        to_early.wait()
        for g in range(groups):
            pack(0, h, g, s0[h])
        if h == 0:
            pl.semaphore_wait(barrier, everyone - 1)
        for g in range(groups):
            copy(0, h, g).start()

    for h in halves:
        @pl.loop(0, lb)
        def _(i):
            first(i, h)[0].start()

    inverse = order_of(masks, groups, jnp.minimum(lane, lb - 1))
    late_v[0:8, :] = packed_exports(masks, lb, inverse)
    word = jnp.zeros((8, 128), jnp.int32)
    for q in range(lb // 8):
        word = word | jnp.where((lane < lb) & (inverse == 8 * q + sublane),
                                lax.shift_left(lane, jnp.full_like(lane, 8 * q)), 0)
    late_v[8:16, :] = folded(word, 1)
    late_v[16:24, :] = inverse
    per = 128 // lb
    start = pl.multiple_of(me // per * 128, 128)
    for o in tiles_of(sc):
        v = cvm[o:o + 8, pl.ds(start, 128)]
        rel = v - me * lb
        near = (rel >= 0) & (rel < lb)
        low = rel & (lb - 1)
        far = jnp.zeros((8, 128), jnp.int32)
        for g, d in enumerate(shifts):
            there = v - lax.rem(me + d + rows, rows) * lb
            at = there & (lb - 1)
            far = jnp.where((there >= 0) & (there < lb),
                            lb + HALO * g + ones_in(mask_row(masks, g) & bits_below(at)), far)
        late_v[24 + o:32 + o, :] = jnp.where(near, low, far)
        late_v[24 + sc + o:32 + sc + o, :] = jnp.where(near, order_of(masks, groups, low), far)
    to_late.start()
    for h in halves:
        @pl.loop(0, lb)
        def _(i):
            first(i, h)[0].wait()

    energies.wait()
    to_late.wait()

    def place(k, j):
        i = j if k == FILTER - 1 else permuted(j)
        own = late[16, j] & (lb - 1) if k == FILTER - 1 else (i if k == 0 else j)
        return i, own

    def feed(k, first_row, accs):
        base = pn if k == 0 else pp
        x = xs[k][0]
        at = [place(k, first_row + u)[0] for u in range(UNROLL)]
        for t in range(sc // 2):
            for m in range(2):
                pair = at[2 * m:2 * m + 2]
                pltpu.matmul_push_rhs(jnp.concatenate(
                    [jnp.concatenate([bm[2 * t, i], bm[2 * t + 1, i]], axis=0) for i in pair],
                    axis=1), t % 2, m)
                for u, i in enumerate(pair):
                    left = jnp.concatenate(
                        [x[late[base + 2 * t + s, shift + i] & (span - 1)] for s in range(2)], axis=1)
                    pltpu.matmul_acc_lhs(accs[m][u], left,
                                         load_staged_rhs=t % 2 if u == 0 else None)

    def settle(k, row, acc, u):
        i, own = place(k, row)
        total = pltpu.matmul_pop(acc)[:, u * bs:(u + 1) * bs]
        total = total + ons[i] * xs[k][0][own].astype(f32)
        if k == 0:
            return filter_scale * total
        prev = xs[0][0][i].astype(f32) if k == 1 else ys[k - 2][0][own]
        return 2.0 * filter_scale * total - prev

    def turn(piece, c):
        return lax.rem(c + (1 - piece // (parts // 2)) * (chunks // 2), chunks)

    def spread(n, h, c):
        bit, m = hops[n]
        piece = mc
        for b in (m & (1 << t) for t in range(m.bit_length())):
            if b:
                piece = flip(piece, b)
        part = out.at[piece * HALVES + h, pl.ds(turn(piece, c) * UNROLL, UNROLL)]
        return pltpu.make_async_remote_copy(
            src_ref=part, dst_ref=part, send_sem=wss.at[n, h, c], recv_sem=wrs.at[n, h, c],
            device_id=(me, flip(mc, bit)), device_id_type=pl.DeviceIdType.MESH)

    firsts = [n for n, (_, m) in enumerate(hops) if m == 0]

    @pl.loop(0, chunks)
    def _(c):
        load(c).wait()

    def keep(k, j, value):
        low = value.astype(bf16)
        if k < FILTER - 1:
            xs[k + 1][0][j] = low
            ys[k][0][j] = value
        else:
            out[mc, j] = low

    def rows_of(k, c):
        return (turn(mc, c) if k == FILTER - 1 else c) * UNROLL

    def chunk(k, c, accs):
        for m in range(2):
            for u in range(2):
                j = rows_of(k, c) + 2 * m + u
                keep(k, j, settle(k, j, accs[m][u], u))

    def filtering(*flat):
        sets = [[flat[4 * q + 2 * m:4 * q + 2 * m + 2] for m in range(2)] for q in range(2)]
        for k in range(FILTER):
            for g in range(groups):
                copy(k, 0, g).wait_recv()
            last = k == FILTER - 1

            def sent(c):
                if last:
                    for n in firsts:
                        spread(n, 0, c).start()

            @pl.loop(0, groups)
            def _(c):
                feed(k, rows_of(k, c), sets[0])
                chunk(k, c, sets[0])
                if not last:
                    pack(k + 1, 0, c, ys[k][0])
                    copy(k + 1, 0, c).start()
                sent(c)

            @pl.loop(groups // 2, chunks // 2)
            def _(cc):
                for q in range(2):
                    feed(k, rows_of(k, 2 * cc + q), sets[q])
                for q in range(2):
                    chunk(k, 2 * cc + q, sets[q])
                for q in range(2):
                    sent(2 * cc + q)

    pl.run_scoped(filtering, *[pltpu.ACC(m)((width, 2 * bs), f32)
                               for _ in range(2) for m in range(2) for _ in range(2)])

    for k in range(FILTER):
        for h in halves:
            for g in range(groups):
                copy(k, h, g).wait_send()

    needs = {n: max(q for q in range(n) if sum(hops[q]) == m)
             for n, (_, m) in enumerate(hops) if m}
    def relay(lo, hi):
        for h in halves:
            @pl.loop(lo, hi)
            def _(c):
                got = set()
                for n in needs:
                    if needs[n] not in got:
                        spread(needs[n], h, c).wait_recv()
                        got.add(needs[n])
                    spread(n, h, c).start()

    def arrive(lo, hi, picked):
        for h in halves:
            @pl.loop(lo, hi)
            def _(c):
                for n in picked:
                    spread(n, h, c).wait_recv()

    top = parts // 2
    leaves = [n for n in range(len(hops)) if n not in needs.values()]
    near = [n for n in leaves if sum(hops[n]) < top]
    other = [n for n in leaves if sum(hops[n]) >= top]
    side = mc // top
    half = lb // 2
    across = top * width

    def tall(q, first_row):
        return jnp.concatenate([out[q, first_row], out[q, first_row + 1]], axis=1)

    def gram_part(phase, part, start, count, *accs):
        one, two = accs[:2], accs[2:]

        @pl.loop(0, count // 8)
        def _(c):
            for m in range(2):
                row = start + c * 8 + 4 * m
                pltpu.matmul_push_rhs(
                    jnp.concatenate([tall(side * top + q, row + r)
                                     for r in (0, 2) for q in range(top)], axis=0),
                    0, m, transpose=True)
                pltpu.matmul_acc_lhs(one[m], tall(part, row), load_staged_rhs=0)
                pltpu.matmul_acc_lhs(two[m], tall(part, row + 2))

        sums = [pltpu.matmul_pop(one[m])[:, :across] + pltpu.matmul_pop(two[m])[:, across:]
                for m in range(2)]
        gp[phase] = sums[0] + sums[1]

    def grams(phase, *where):
        pl.run_scoped(functools.partial(gram_part, phase, *where),
                      *[pltpu.ACC(m)((width, 2 * across), f32) for _ in range(2) for m in range(2)])

    def part_to(phase, d):
        to = lax.rem(me + d, rows)
        lo = pl.multiple_of(to * rps, rps)
        return to, pltpu.make_async_remote_copy(
            src_ref=gp.at[phase, pl.ds(lo, rps)], dst_ref=rb.at[phase, d],
            send_sem=pss.at[phase, d], recv_sem=prs.at[phase, d], device_id=(to, mc),
            device_id_type=pl.DeviceIdType.MESH)

    def part_in(phase, d):
        return pltpu.make_async_remote_copy(
            src_ref=gp.at[phase, pl.ds(0, rps)], dst_ref=rb.at[phase, d],
            send_sem=pss.at[phase, d], recv_sem=prs.at[phase, d],
            device_id=(lax.rem(me + 1, rows), mc), device_id_type=pl.DeviceIdType.MESH)

    def only(cond, run):
        if reducers == rows:
            run()
        else:
            pl.when(cond)(run)

    def scatter(phase):
        @pl.loop(1, rows)
        def _(d):
            to, c = part_to(phase, d)
            only(to < reducers, lambda: c.start())

    def spot(phase, sender):
        part = lax.rem(sender, parts)
        block = part // top
        if phase == 1:
            part = flip(part, top)
        lo = pl.multiple_of((part * reducers + sender // parts) * rps, rps)
        return pl.ds(lo, rps), pl.ds(pl.multiple_of(block * across, across), across)

    def all_to(phase, e, sender):
        to = lax.rem(linear + e, everyone)
        return pltpu.make_async_remote_copy(
            src_ref=gs.at[phase], dst_ref=gram.at[spot(phase, sender)], send_sem=ass.at[phase, e],
            recv_sem=ars.at[phase, e], device_id=(to // parts, lax.rem(to, parts)),
            device_id_type=pl.DeviceIdType.MESH)

    def reduce(phase):
        lo = pl.multiple_of(me * rps, rps)
        total = gp[phase, pl.ds(lo, rps)]
        for d in range(1, rows):
            part_in(phase, d).wait_recv()
            total = total + rb[phase, d]
        gs[phase] = total
        gram[spot(phase, linear)] = total

        @pl.loop(1, everyone)
        def _(e):
            all_to(phase, e, linear).start()

    def gathered(phase):
        @pl.loop(1, everyone)
        def _(e):
            sender = lax.rem(linear - e + everyone, everyone)
            only(sender // parts < reducers, lambda: all_to(phase, e, sender).wait_recv())

    arrive(0, chunks, near)
    grams(0, mc, 0, lb)
    scatter(0)
    relay(0, chunks // 2)
    grams(1, flip(mc, top), side * half, half)
    scatter(1)
    only(me < reducers, functools.partial(reduce, 0))
    only(me < reducers, functools.partial(reduce, 1))
    relay(chunks // 2, chunks)
    gathered(0)
    arrive(0, chunks, other)
    keep_all = pltpu.make_async_copy(out, stored, osem.at[0])
    keep_all.start()
    keep_gram = pltpu.make_async_copy(gram, gram_out, osem.at[1])

    def between():
        gathered(1)
        keep_gram.start()

    eliminate([gram[8 * t:8 * t + 8, :across] for t in range(across // 8)], first_up, first_low,
              between)
    keep_first = [pltpu.make_async_copy(first_up, up_out, osem.at[2]),
                  pltpu.make_async_copy(first_low, low_out, osem.at[3])]
    for kept in keep_first:
        kept.start()
    for h in halves:
        @pl.loop(0, chunks)
        def _(c):
            for n in range(len(hops)):
                spread(n, h, c).wait_send()

    for phase in range(2):
        @pl.loop(1, rows)
        def _(d):
            to, c = part_to(phase, d)
            only(to < reducers, lambda: c.wait_send())

        @pl.loop(1, everyone)
        def _(e):
            only(me < reducers, lambda: all_to(phase, e, linear).wait_send())

    for kept in (keep_all, keep_gram, *keep_first):
        kept.wait()


def filtered(subspace, onsite, blocks, cols):
    rows, parts = lax.axis_size("row"), lax.axis_size("col")
    everyone, hops = rows * parts, len(hops_of(parts))
    width = subspace.shape[0]
    sc, lb, bs, _ = blocks.shape
    groups = len(shifts_of(rows))
    assert lb in (8, 16, 32) and sc >= 8
    ext = pl.next_power_of_2(lb + groups * HALO)
    vm, dma = pltpu.VMEM, pltpu.SemaphoreType.DMA
    full, hw = parts * width, width // HALVES
    half = full // 2
    rps = slice_of(width, rows)
    return pl.pallas_call(
        functools.partial(filter_kernel, rows, parts, lb, sc),
        out_shape=(jax.ShapeDtypeStruct((parts * HALVES, lb, hw, bs), bf16),
                   jax.ShapeDtypeStruct((full, full), f32)) + (jax.ShapeDtypeStruct((half, half), f32),) * 2,
        in_specs=[pl.BlockSpec(memory_space=pl.ANY)] * 4,
        out_specs=[pl.BlockSpec(memory_space=pl.ANY)] * 4,
        scratch_shapes=[vm((sc, lb, bs, bs), bf16)]
        + [vm((ext, hw, bs), bf16)] * (FILTER * HALVES)
        + [vm((groups * HALO, hw, bs), bf16)] * (FILTER * HALVES)
        + [vm((lb, hw, bs), f32)] * ((FILTER - 1) * HALVES)
        + [vm((lb, hw, bs), bf16)] * HALVES
        + [vm((parts * HALVES, lb, hw, bs), bf16), vm((lb, 1, bs), f32), vm(cols.shape[::-1], jnp.int32),
           vm((8, 128), jnp.int32), vm((24 + 2 * sc, 128), jnp.int32),
           pltpu.SMEM((8, 128), jnp.int32), pltpu.SMEM((24 + 2 * sc, 128), jnp.int32)]
        + [vm((2, width, half), f32), vm((2, rps, half), f32), vm((2, rows, rps, half), f32)]
        + [dma((lb // UNROLL,)), dma((HALVES, lb)), dma((HALVES, lb)),
           dma((FILTER, HALVES, groups)), dma((FILTER, HALVES, groups)),
           dma((hops, HALVES, lb // UNROLL)), dma((hops, HALVES, lb // UNROLL)),
           dma((2, rows)), dma((2, rows)), dma((2, everyone)), dma((2, everyone)), dma((4,)), dma((4,)),
           vm((full, full), f32), vm((half, half), f32), vm((half, half), f32)],
        compiler_params=pltpu.CompilerParams(
            collective_id=0, has_side_effects=True, vmem_limit_bytes=56 * 1024 * 1024),
        name="filter",
    )(cols.T, subspace, onsite.reshape(lb, 1, bs), blocks)


def eliminate(a, up, low, between=None):
    tiles = len(a)
    n = 8 * tiles
    sub = lax.broadcasted_iota(jnp.int32, (8, n), 0)
    lane = lax.broadcasted_iota(jnp.int32, (8, n), 1)
    b = [jnp.where(lane == sub + 8 * t, 1.0, 0.0).astype(f32) for t in range(tiles)]

    def row(v, q):
        return jnp.broadcast_to(v[q:q + 1, :], (8, n))

    for p in range(tiles):
        if between and p == 3 * tiles // 4:
            between()
        cols = {t: [jnp.broadcast_to(a[t][:, 8 * p + q:8 * p + q + 1], (8, n)) for q in range(8)]
                for t in range(p, tiles)}
        pivots = jnp.ones((8, n), f32)
        for q in range(8):
            pivot = row(cols[p][q], q)
            pivots = jnp.where(sub == q, pivot, pivots)
            inverse = 1.0 / pivot
            right = [row(cols[p][k], q) for k in range(8)]
            arow, brow = row(a[p], q), row(b[p], q)
            for t in range(p, tiles):
                m = cols[t][q] * inverse
                if t == p:
                    m = jnp.where(sub > q, m, 0.0)
                for k in range(q + 1, 8):
                    cols[t][k] = cols[t][k] - m * right[k]
                a[t] = a[t] - m * arow
                b[t] = b[t] - m * brow
        scale = lax.rsqrt(pivots)
        up[8 * p:8 * p + 8, :] = jnp.where(lane >= sub + 8 * p, a[p] * scale, 0.0)
        low[8 * p:8 * p + 8, :] = b[p] * scale


def finish_kernel(root, col, stored, gram_in, up_in, low_in, basis_out, factor_out,
                  basis, factor, up, low, inv, gram, first_up, first_low, whole, sem):
    operands = [pltpu.make_async_copy(*pair, sem.at[6 + n]) for n, pair in enumerate(
        ((low_in, first_low), (gram_in, gram), (up_in, first_up)))]
    for operand in operands:
        operand.start()
    fetch = pltpu.make_async_copy(stored, whole, sem.at[0])
    fetch.start()
    parts, lb, _, bs = whole.shape
    width = basis.shape[0]
    full = gram.shape[0]
    half = full // 2
    exact = functools.partial(lax.dot_general, precision=lax.Precision.HIGHEST,
                              preferred_element_type=f32)
    nn, tn = (((1,), (0,)), ((), ())), (((0,), (0,)), ((), ()))
    operands[0].wait()
    operands[1].wait()
    corner = gram[:half, half:] + gram[half:, :half].T
    across = exact(first_low[...], corner, nn)
    rest = gram[half:, half:] - exact(across, across, tn)
    eliminate([rest[8 * t:8 * t + 8, :] for t in range(half // 8)], up, low)
    factor[half:, :half] = jnp.zeros((half, half), f32)
    inv[:half, half:] = jnp.zeros((half, half), f32)
    inv[:half, :half] = first_low[...]
    inv[half:, half:] = low[...]
    inv[half:, :half] = -exact(low[...], exact(across, first_low[...], tn), nn)
    operands[2].wait()
    factor[:half, :half] = first_up[...] * (1.0 / root)
    factor[:half, half:] = across * (1.0 / root)
    factor[half:, half:] = up[...] * (1.0 / root)
    put = [pltpu.make_async_copy(factor, factor_out, sem.at[1])]
    put[0].start()

    mine = inv[pl.ds(pl.multiple_of(col[0] * width, width), width), :] * root
    high = mine.astype(bf16)
    rest = mine - high.astype(f32)
    left = jnp.concatenate([high, rest.astype(bf16)], axis=0)

    fetch.wait()
    every = lb // 4
    for k in range(lb):
        right = jnp.concatenate([whole[q, k] for q in range(parts)], axis=0)
        r = jnp.dot(left, right, preferred_element_type=f32)
        basis[:, k * bs:(k + 1) * bs] = r[:width] + r[width:]
        if k % every == every - 1:
            cut = pl.ds((k + 1 - every) * bs, every * bs)
            put.append(pltpu.make_async_copy(basis.at[:, cut], basis_out.at[:, cut],
                                             sem.at[2 + k // every]))
            put[-1].start()
    for copy in put:
        copy.wait()


def body(subspace, onsite, blocks, cols):
    row_count = lax.axis_size("row")
    part_width, local_rows = subspace.shape
    whole, gram, first_up, first_low = filtered(subspace, onsite, blocks, cols)
    full = gram.shape[0]
    half = full // 2
    root = math.sqrt(row_count * local_rows)
    vm = pltpu.VMEM
    return pl.pallas_call(
        functools.partial(finish_kernel, root),
        out_shape=(jax.ShapeDtypeStruct((part_width, local_rows), f32),
                   jax.ShapeDtypeStruct((full, full), f32)),
        in_specs=[pl.BlockSpec(memory_space=pltpu.SMEM), *[pl.BlockSpec(memory_space=pltpu.HBM)] * 4],
        out_specs=[pl.BlockSpec(memory_space=pl.ANY)] * 2,
        scratch_shapes=[vm((part_width, local_rows), f32), vm((full, full), f32),
                        vm((half, half), f32), vm((half, half), f32), vm((full, full), f32),
                        vm((full, full), f32), vm((half, half), f32), vm((half, half), f32),
                        vm(whole.shape, bf16), pltpu.SemaphoreType.DMA((9,))],
        compiler_params=pltpu.CompilerParams(vmem_limit_bytes=60 * 1024 * 1024),
        name="finish",
    )(lax.axis_index("col").astype(jnp.int32).reshape(1), whole, gram, first_up, first_low)


def solution(mesh):
    in_specs = (P("col", "row"), P("row"), P(None, "row", None, None), P())
    out_specs = (P("col", "row"), P())
    return jax.shard_map(body, mesh=mesh, in_specs=in_specs, out_specs=out_specs, check_vma=False)
```

```python
import functools
import math

import jax
import jax.numpy as jnp
from jax import lax
from jax.experimental import pallas as pl
from jax.experimental.pallas import tpu as pltpu
from jax.sharding import PartitionSpec as P

HALO = 4
FILTER = 4
UNROLL = 4
HALVES = 1
filter_scale = 0.4
f32 = jnp.float32
bf16 = jnp.bfloat16


def shifts_of(rows):
    return (1, -1, 2, rows // 2)


def bits_below(k):
    return lax.shift_left(jnp.ones_like(k), k) - 1


def ones_in(x):
    return lax.population_count(x)


def folded(x, axis):
    step = x.shape[axis] // 2
    while step:
        x = x | pltpu.roll(x, step, axis)
        step //= 2
    return x


def tiles_of(sc):
    return list(range(0, sc - 7, 8)) + ([sc - 8] if sc % 8 else [])


def masks_of(cvm, rows, me, lb, sc):
    shifts = shifts_of(rows)
    groups = len(shifts)
    lane = lax.broadcasted_iota(jnp.int32, (8, 128), 1)
    sub = lax.broadcasted_iota(jnp.int32, (8, 128), 0)
    per = 128 // lb

    def picked(device, owners):
        start = pl.multiple_of(device // per * 128, 128)
        live = lane // lb == lax.rem(device, per)
        found = [jnp.zeros((8, 128), jnp.int32) for _ in owners]
        for o in tiles_of(sc):
            v = cvm[o:o + 8, pl.ds(start, 128)]
            for n, owner in enumerate(owners):
                rel = v - owner * lb
                hit = live & (rel >= 0) & (rel < lb)
                found[n] = found[n] | jnp.where(
                    hit, lax.shift_left(jnp.ones_like(rel), rel & (lb - 1)), 0)
        return found

    found = picked(me, [lax.rem(me + d + rows, rows) for d in shifts])
    for d in shifts:
        found += picked(lax.rem(me - d + rows, rows), [me])
    both = jnp.zeros((8, 128), jnp.int32)
    for n, x in enumerate(found):
        both = jnp.where(sub == n, folded(x, 0), both)
    assert groups == 4
    return folded(both, 1)


def mask_row(masks, n):
    return jnp.broadcast_to(masks[n:n + 1, :], (8, 128))


def byte_of(word, n, limit):
    return lax.shift_right_logical(word, 8 * n) & (limit - 1)


def packed_exports(masks, lb, names):
    k = lax.broadcasted_iota(jnp.int32, (8, 128), 1)
    low = jnp.minimum(k, lb - 1)
    hit = (k < lb) & ((lax.shift_right_logical(masks, low) & 1) == 1)
    rank = ones_in(masks & bits_below(low))
    word = jnp.zeros((8, 128), jnp.int32)
    for m in range(HALO):
        word = word | jnp.where(hit & (rank == m), lax.shift_left(names, jnp.full_like(names, 8 * m)), 0)
    return folded(word, 1)


def order_of(masks, groups, at):
    taken = jnp.zeros((8, 128), jnp.int32)
    base = jnp.zeros((8, 128), jnp.int32)
    place = jnp.zeros((8, 128), jnp.int32)
    below = bits_below(at)
    for g in range(groups + 1):
        left = ~taken
        mine = left if g == groups else mask_row(masks, groups + g) & left
        here = (lax.shift_right_logical(mine, at) & 1) == 1
        place = jnp.where(here, base + ones_in(mine & below), place)
        base = base + ones_in(mine)
        taken = taken | mine
    return place


def flip(c, bit):
    return c + bit - 2 * bit * lax.rem(c // bit, 2)


def hops_of(parts):
    hops, held, bit = [], [0], parts // 2
    while bit:
        hops += [(bit, m) for m in held]
        held += [m + bit for m in held]
        bit //= 2
    return hops


def slice_of(width, rows):
    return max(8, width // rows)


def filter_kernel(rows, parts, lb, sc, cols, sub, ons_in, blk, stored, gram_out, up_out,
                  low_out, bm, *refs):
    refs = list(refs)
    take = lambda n: [refs.pop(0) for _ in range(n)]
    halves = range(HALVES)
    xs = [take(HALVES) for _ in range(FILTER)]
    snds = [take(HALVES) for _ in range(FILTER)]
    ys = [take(HALVES) for _ in range(FILTER - 1)]
    s0 = take(HALVES)
    (out, ons, cvm, early_v, late_v, early, late, gp, gs, rb, bsem, xsem, csem, ssem, rsem,
     wss, wrs, pss, prs, ass, ars, tsem, osem, gram, first_up, first_low) = refs
    me = lax.axis_index("row")
    mc = lax.axis_index("col")
    everyone = rows * parts
    width = sub.shape[0]
    hw = width // HALVES
    hops = hops_of(parts)
    rps = slice_of(width, rows)
    reducers = width // rps
    shifts = shifts_of(rows)
    groups = len(shifts)
    bs = blk.shape[-1]
    chunks = lb // UNROLL

    def load(c):
        part = pl.ds(c * UNROLL, UNROLL)
        return pltpu.make_async_copy(blk.at[:, part], bm.at[:, part], bsem.at[c])

    def first(i, h):
        cut = sub.at[pl.ds(h * hw, hw), pl.ds(pl.multiple_of(i * bs, bs), bs)]
        return (pltpu.make_async_copy(cut, xs[0][h].at[i], xsem.at[h, i]),
                pltpu.make_async_copy(cut, s0[h].at[i], csem.at[h, i]))

    named = pltpu.make_async_copy(cols, cvm, tsem.at[0])
    named.start()
    barrier = pltpu.get_barrier_semaphore()

    def wrapped(x, n):
        return jnp.where(x >= n, x - n, x)

    part_at = [wrapped(mc + j, parts) for j in range(parts)]

    def greet(d, first_part=0):
        for j in range(first_part, parts):
            pl.semaphore_signal(barrier, inc=1, device_id=(wrapped(me + d, rows), part_at[j]),
                                device_id_type=pl.DeviceIdType.MESH)

    pl.loop(1, rows)(greet)
    greet(0, 1)

    for h in halves:
        @pl.loop(0, lb)
        def _(i):
            first(i, h)[1].start()

    energies = pltpu.make_async_copy(ons_in, ons, tsem.at[1])
    energies.start()

    @pl.loop(0, chunks)
    def _(c):
        load(c).start()

    named.wait()
    masks = masks_of(cvm, rows, me, lb, sc)
    lane = lax.broadcasted_iota(jnp.int32, (8, 128), 1)
    sublane = lax.broadcasted_iota(jnp.int32, (8, 128), 0)
    early_v[...] = packed_exports(masks, lb, lane)
    to_early = pltpu.make_async_copy(early_v, early, tsem.at[2])
    to_early.start()

    to_late = pltpu.make_async_copy(late_v, late, tsem.at[3])
    shift = lax.rem(me, 128 // lb) * lb
    pn, pp, span = 24, 24 + sc, xs[0][0].shape[0]

    def export(k, g, m):
        return byte_of(early[groups + g, 0] if k == 0 else late[groups + g, 0], m, lb)

    def permuted(j):
        return byte_of(late[8 + lax.rem(j, 8), 0], j // 8, lb)

    def offset_of(g):
        if isinstance(g, int):
            return shifts[g]
        found = shifts[-1]
        for n in range(groups - 1):
            found = jnp.where(g == n, shifts[n], found)
        return found

    def copy(k, h, g):
        return pltpu.make_async_remote_copy(
            src_ref=snds[k][h].at[pl.ds(g * HALO, HALO)],
            dst_ref=xs[k][h].at[pl.ds(lb + g * HALO, HALO)],
            send_sem=ssem.at[k, h, g], recv_sem=rsem.at[k, h, g],
            device_id=(lax.rem(me - offset_of(g) + rows, rows), mc),
            device_id_type=pl.DeviceIdType.MESH)

    def pack(k, h, g, source):
        for m in range(HALO):
            snds[k][h][g * HALO + m] = source[export(k, g, m)].astype(bf16)

    for h in halves:
        @pl.loop(0, lb)
        def _(i):
            first(i, h)[1].wait()

        to_early.wait()
        for g in range(groups):
            pack(0, h, g, s0[h])
        if h == 0:
            pl.semaphore_wait(barrier, everyone - 1)
        for g in range(groups):
            copy(0, h, g).start()

    for h in halves:
        @pl.loop(0, lb)
        def _(i):
            first(i, h)[0].start()

    inverse = order_of(masks, groups, jnp.minimum(lane, lb - 1))
    late_v[0:8, :] = packed_exports(masks, lb, inverse)
    word = jnp.zeros((8, 128), jnp.int32)
    for q in range(lb // 8):
        word = word | jnp.where((lane < lb) & (inverse == 8 * q + sublane),
                                lax.shift_left(lane, jnp.full_like(lane, 8 * q)), 0)
    late_v[8:16, :] = folded(word, 1)
    late_v[16:24, :] = inverse
    per = 128 // lb
    start = pl.multiple_of(me // per * 128, 128)
    for o in tiles_of(sc):
        v = cvm[o:o + 8, pl.ds(start, 128)]
        rel = v - me * lb
        near = (rel >= 0) & (rel < lb)
        low = rel & (lb - 1)
        far = jnp.zeros((8, 128), jnp.int32)
        for g, d in enumerate(shifts):
            there = v - lax.rem(me + d + rows, rows) * lb
            at = there & (lb - 1)
            far = jnp.where((there >= 0) & (there < lb),
                            lb + HALO * g + ones_in(mask_row(masks, g) & bits_below(at)), far)
        late_v[24 + o:32 + o, :] = jnp.where(near, low, far)
        late_v[24 + sc + o:32 + sc + o, :] = jnp.where(near, order_of(masks, groups, low), far)
    to_late.start()
    for h in halves:
        @pl.loop(0, lb)
        def _(i):
            first(i, h)[0].wait()

    energies.wait()
    to_late.wait()

    def place(k, j):
        i = j if k == FILTER - 1 else permuted(j)
        own = late[16, j] & (lb - 1) if k == FILTER - 1 else (i if k == 0 else j)
        return i, own

    def feed(k, first_row, accs):
        base = pn if k == 0 else pp
        x = xs[k][0]
        at = [place(k, first_row + u)[0] for u in range(UNROLL)]
        for t in range(sc // 2):
            for m in range(2):
                pair = at[2 * m:2 * m + 2]
                pltpu.matmul_push_rhs(jnp.concatenate(
                    [jnp.concatenate([bm[2 * t, i], bm[2 * t + 1, i]], axis=0) for i in pair],
                    axis=1), t % 2, m)
                for u, i in enumerate(pair):
                    left = jnp.concatenate(
                        [x[late[base + 2 * t + s, shift + i] & (span - 1)] for s in range(2)], axis=1)
                    pltpu.matmul_acc_lhs(accs[m][u], left,
                                         load_staged_rhs=t % 2 if u == 0 else None)

    def settle(k, row, acc, u):
        i, own = place(k, row)
        total = pltpu.matmul_pop(acc)[:, u * bs:(u + 1) * bs]
        total = total + ons[i] * xs[k][0][own].astype(f32)
        if k == 0:
            return filter_scale * total
        prev = xs[0][0][i].astype(f32) if k == 1 else ys[k - 2][0][own]
        return 2.0 * filter_scale * total - prev

    def turn(piece, c):
        return lax.rem(c + (1 - piece // (parts // 2)) * (chunks // 2), chunks)

    def spread(n, h, c):
        bit, m = hops[n]
        piece = mc
        for b in (m & (1 << t) for t in range(m.bit_length())):
            if b:
                piece = flip(piece, b)
        part = out.at[piece * HALVES + h, pl.ds(turn(piece, c) * UNROLL, UNROLL)]
        return pltpu.make_async_remote_copy(
            src_ref=part, dst_ref=part, send_sem=wss.at[n, h, c], recv_sem=wrs.at[n, h, c],
            device_id=(me, flip(mc, bit)), device_id_type=pl.DeviceIdType.MESH)

    firsts = [n for n, (_, m) in enumerate(hops) if m == 0]

    @pl.loop(0, chunks)
    def _(c):
        load(c).wait()

    def keep(k, j, value):
        low = value.astype(bf16)
        if k < FILTER - 1:
            xs[k + 1][0][j] = low
            ys[k][0][j] = value
        else:
            out[mc, j] = low

    def rows_of(k, c):
        return (turn(mc, c) if k == FILTER - 1 else c) * UNROLL

    def chunk(k, c, accs):
        for m in range(2):
            for u in range(2):
                j = rows_of(k, c) + 2 * m + u
                keep(k, j, settle(k, j, accs[m][u], u))

    def filtering(*flat):
        sets = [[flat[4 * q + 2 * m:4 * q + 2 * m + 2] for m in range(2)] for q in range(2)]
        for k in range(FILTER):
            for g in range(groups):
                copy(k, 0, g).wait_recv()
            last = k == FILTER - 1

            def sent(c):
                if last:
                    for n in firsts:
                        spread(n, 0, c).start()

            @pl.loop(0, groups)
            def _(c):
                feed(k, rows_of(k, c), sets[0])
                chunk(k, c, sets[0])
                if not last:
                    pack(k + 1, 0, c, ys[k][0])
                    copy(k + 1, 0, c).start()
                sent(c)

            @pl.loop(groups // 2, chunks // 2)
            def _(cc):
                for q in range(2):
                    feed(k, rows_of(k, 2 * cc + q), sets[q])
                for q in range(2):
                    chunk(k, 2 * cc + q, sets[q])
                for q in range(2):
                    sent(2 * cc + q)

    pl.run_scoped(filtering, *[pltpu.ACC(m)((width, 2 * bs), f32)
                               for _ in range(2) for m in range(2) for _ in range(2)])


    needs = {n: max(q for q in range(n) if sum(hops[q]) == m)
             for n, (_, m) in enumerate(hops) if m}
    def relay(lo, hi):
        for h in halves:
            @pl.loop(lo, hi)
            def _(c):
                got = set()
                for n in needs:
                    if needs[n] not in got:
                        spread(needs[n], h, c).wait_recv()
                        got.add(needs[n])
                    spread(n, h, c).start()

    def arrive(lo, hi, picked):
        for h in halves:
            @pl.loop(lo, hi)
            def _(c):
                for n in picked:
                    spread(n, h, c).wait_recv()

    top = parts // 2
    leaves = [n for n in range(len(hops)) if n not in needs.values()]
    near = [n for n in leaves if sum(hops[n]) < top]
    other = [n for n in leaves if sum(hops[n]) >= top]
    side = mc // top
    half = lb // 2
    across = top * width

    def tall(q, first_row):
        return jnp.concatenate([out[q, first_row], out[q, first_row + 1]], axis=1)

    def gram_part(phase, part, row_of, count, ready, *accs):
        one, two = accs[:2], accs[2:]

        @pl.loop(0, count // 8)
        def _(c):
            if ready:
                ready(c)
            for m in range(2):
                row = row_of(c) + 4 * m
                pltpu.matmul_push_rhs(
                    jnp.concatenate([tall(side * top + q, row + r)
                                     for r in (0, 2) for q in range(top)], axis=0),
                    0, m, transpose=True)
                pltpu.matmul_acc_lhs(one[m], tall(part, row), load_staged_rhs=0)
                pltpu.matmul_acc_lhs(two[m], tall(part, row + 2))

        sums = [pltpu.matmul_pop(one[m])[:, :across] + pltpu.matmul_pop(two[m])[:, across:]
                for m in range(2)]
        gp[phase] = sums[0] + sums[1]

    def grams(phase, *where):
        pl.run_scoped(functools.partial(gram_part, phase, *where),
                      *[pltpu.ACC(m)((width, 2 * across), f32) for _ in range(2) for m in range(2)])

    def part_to(phase, d):
        to = lax.rem(me + d, rows)
        lo = pl.multiple_of(to * rps, rps)
        return to, pltpu.make_async_remote_copy(
            src_ref=gp.at[phase, pl.ds(lo, rps)], dst_ref=rb.at[phase, d],
            send_sem=pss.at[phase, d], recv_sem=prs.at[phase, d], device_id=(to, mc),
            device_id_type=pl.DeviceIdType.MESH)

    def part_in(phase, d):
        return pltpu.make_async_remote_copy(
            src_ref=gp.at[phase, pl.ds(0, rps)], dst_ref=rb.at[phase, d],
            send_sem=pss.at[phase, d], recv_sem=prs.at[phase, d],
            device_id=(lax.rem(me + 1, rows), mc), device_id_type=pl.DeviceIdType.MESH)

    def only(cond, run):
        if reducers == rows:
            run()
        else:
            pl.when(cond)(run)

    def scatter(phase):
        @pl.loop(1, rows)
        def _(d):
            to, c = part_to(phase, d)
            only(to < reducers, lambda: c.start())

    def spot(phase, row, part):
        block = part // top
        if phase == 1:
            part = flip(part, top)
        lo = pl.multiple_of((part * reducers + row) * rps, rps)
        return pl.ds(lo, rps), pl.ds(pl.multiple_of(block * across, across), across)

    def all_to(phase, d, j, place):
        return pltpu.make_async_remote_copy(
            src_ref=gs.at[phase], dst_ref=gram.at[place], send_sem=ass.at[phase, d * parts + j],
            recv_sem=ars.at[phase, d * parts + j], device_id=(wrapped(me + d, rows), part_at[j]),
            device_id_type=pl.DeviceIdType.MESH)

    def reduce(phase):
        lo = pl.multiple_of(me * rps, rps)
        total = gp[phase, pl.ds(lo, rps)]
        for d in range(1, rows):
            part_in(phase, d).wait_recv()
            total = total + rb[phase, d]
        gs[phase] = total
        place = spot(phase, me, mc)
        gram[place] = total

        def send(d, first_part=0):
            for j in range(first_part, parts):
                all_to(phase, d, j, place).start()

        pl.loop(rows // 4, 3 * rows // 4 + 1)(send)
        pl.loop(3 * rows // 4 + 1, rows)(send)
        pl.loop(1, rows // 4)(send)
        send(0, 1)

    def gathered(phase):
        def arrived(d, first_part=0):
            row = wrapped(me - d + rows, rows)

            def run():
                for j in range(first_part, parts):
                    place = spot(phase, row, wrapped(mc - j + parts, parts))
                    all_to(phase, d, j, place).wait_recv()

            only(row < reducers, run)

        arrived(0, 1)
        pl.loop(1, rows)(arrived)

    def passed_on(phase):
        place = spot(phase, me, mc)

        def left(d, first_part=0):
            for j in range(first_part, parts):
                all_to(phase, d, j, place).wait_send()

        left(0, 1)
        pl.loop(1, rows)(left)


    def beside(c):
        for q in range(2):
            for n in near:
                spread(n, 0, 2 * c + q).wait_recv()

    grams(0, mc, lambda c: rows_of(FILTER - 1, 2 * c), lb, beside)
    scatter(0)
    relay(0, chunks // 2)
    grams(1, flip(mc, top), lambda c: side * half + 8 * c, half, None)
    scatter(1)
    only(me < reducers, functools.partial(reduce, 0))
    only(me < reducers, functools.partial(reduce, 1))
    relay(chunks // 2, chunks)
    gathered(0)
    arrive(0, chunks, other)
    keep_all = pltpu.make_async_copy(out, stored, osem.at[0])
    keep_all.start()
    keep_gram = pltpu.make_async_copy(gram, gram_out, osem.at[1])

    def between():
        gathered(1)
        keep_gram.start()

    eliminate([gram[8 * t:8 * t + 8, :across] for t in range(across // 8)], first_up, first_low,
              between)
    keep_first = [pltpu.make_async_copy(first_up, up_out, osem.at[2]),
                  pltpu.make_async_copy(first_low, low_out, osem.at[3])]
    for kept in keep_first:
        kept.start()
    for h in halves:
        @pl.loop(0, chunks)
        def _(c):
            for n in range(len(hops)):
                spread(n, h, c).wait_send()

    for k in range(FILTER):
        for h in halves:
            for g in range(groups):
                copy(k, h, g).wait_send()

    for phase in range(2):
        @pl.loop(1, rows)
        def _(d):
            to, c = part_to(phase, d)
            only(to < reducers, lambda: c.wait_send())

        only(me < reducers, functools.partial(passed_on, phase))

    for kept in (keep_all, keep_gram, *keep_first):
        kept.wait()


def filtered(subspace, onsite, blocks, cols):
    rows, parts = lax.axis_size("row"), lax.axis_size("col")
    everyone, hops = rows * parts, len(hops_of(parts))
    width = subspace.shape[0]
    sc, lb, bs, _ = blocks.shape
    groups = len(shifts_of(rows))
    assert lb in (8, 16, 32) and sc >= 8
    ext = pl.next_power_of_2(lb + groups * HALO)
    vm, dma = pltpu.VMEM, pltpu.SemaphoreType.DMA
    full, hw = parts * width, width // HALVES
    half = full // 2
    rps = slice_of(width, rows)
    return pl.pallas_call(
        functools.partial(filter_kernel, rows, parts, lb, sc),
        out_shape=(jax.ShapeDtypeStruct((parts * HALVES, lb, hw, bs), bf16),
                   jax.ShapeDtypeStruct((full, full), f32)) + (jax.ShapeDtypeStruct((half, half), f32),) * 2,
        in_specs=[pl.BlockSpec(memory_space=pl.ANY)] * 4,
        out_specs=[pl.BlockSpec(memory_space=pl.ANY)] * 4,
        scratch_shapes=[vm((sc, lb, bs, bs), bf16)]
        + [vm((ext, hw, bs), bf16)] * (FILTER * HALVES)
        + [vm((groups * HALO, hw, bs), bf16)] * (FILTER * HALVES)
        + [vm((lb, hw, bs), f32)] * ((FILTER - 1) * HALVES)
        + [vm((lb, hw, bs), bf16)] * HALVES
        + [vm((parts * HALVES, lb, hw, bs), bf16), vm((lb, 1, bs), f32), vm(cols.shape[::-1], jnp.int32),
           vm((8, 128), jnp.int32), vm((24 + 2 * sc, 128), jnp.int32),
           pltpu.SMEM((8, 128), jnp.int32), pltpu.SMEM((24 + 2 * sc, 128), jnp.int32)]
        + [vm((2, width, half), f32), vm((2, rps, half), f32), vm((2, rows, rps, half), f32)]
        + [dma((lb // UNROLL,)), dma((HALVES, lb)), dma((HALVES, lb)),
           dma((FILTER, HALVES, groups)), dma((FILTER, HALVES, groups)),
           dma((hops, HALVES, lb // UNROLL)), dma((hops, HALVES, lb // UNROLL)),
           dma((2, rows)), dma((2, rows)), dma((2, everyone)), dma((2, everyone)), dma((4,)), dma((4,)),
           vm((full, full), f32), vm((half, half), f32), vm((half, half), f32)],
        compiler_params=pltpu.CompilerParams(
            collective_id=0, has_side_effects=True, vmem_limit_bytes=56 * 1024 * 1024),
        name="filter",
    )(cols.T, subspace, onsite.reshape(lb, 1, bs), blocks)


def eliminate(a, up, low, between=None):
    tiles = len(a)
    n = 8 * tiles
    sub = lax.broadcasted_iota(jnp.int32, (8, n), 0)
    lane = lax.broadcasted_iota(jnp.int32, (8, n), 1)
    b = [jnp.where(lane == sub + 8 * t, 1.0, 0.0).astype(f32) for t in range(tiles)]

    def row(v, q):
        return jnp.broadcast_to(v[q:q + 1, :], (8, n))

    for p in range(tiles):
        if between and p == 3 * tiles // 4:
            between()
        cols = {t: [jnp.broadcast_to(a[t][:, 8 * p + q:8 * p + q + 1], (8, n)) for q in range(8)]
                for t in range(p, tiles)}
        pivots = jnp.ones((8, n), f32)
        for q in range(8):
            pivot = row(cols[p][q], q)
            pivots = jnp.where(sub == q, pivot, pivots)
            inverse = 1.0 / pivot
            right = [row(cols[p][k], q) for k in range(8)]
            arow, brow = row(a[p], q), row(b[p], q)
            for t in range(p, tiles):
                m = cols[t][q] * inverse
                if t == p:
                    m = jnp.where(sub > q, m, 0.0)
                for k in range(q + 1, 8):
                    cols[t][k] = cols[t][k] - m * right[k]
                a[t] = a[t] - m * arow
                b[t] = b[t] - m * brow
        scale = lax.rsqrt(pivots)
        up[8 * p:8 * p + 8, :] = jnp.where(lane >= sub + 8 * p, a[p] * scale, 0.0)
        low[8 * p:8 * p + 8, :] = b[p] * scale


def finish_kernel(root, stored, gram_in, up_in, low_in, basis_out, factor_out,
                  basis, factor, up, low, inv, gram, first_up, first_low, whole, sem):
    operands = [pltpu.make_async_copy(*pair, sem.at[6 + n]) for n, pair in enumerate(
        ((low_in, first_low), (gram_in, gram), (up_in, first_up)))]
    for operand in operands:
        operand.start()
    fetch = pltpu.make_async_copy(stored, whole, sem.at[0])
    fetch.start()
    parts, lb, _, bs = whole.shape
    width = basis.shape[0]
    full = gram.shape[0]
    half = full // 2
    exact = functools.partial(lax.dot_general, precision=lax.Precision.HIGHEST,
                              preferred_element_type=f32)
    nn, tn = (((1,), (0,)), ((), ())), (((0,), (0,)), ((), ()))
    operands[0].wait()
    operands[1].wait()
    corner = gram[:half, half:] + gram[half:, :half].T
    across = exact(first_low[...], corner, nn)
    rest = gram[half:, half:] - exact(across, across, tn)
    eliminate([rest[8 * t:8 * t + 8, :] for t in range(half // 8)], up, low)
    factor[half:, :half] = jnp.zeros((half, half), f32)
    inv[:half, half:] = jnp.zeros((half, half), f32)
    inv[:half, :half] = first_low[...]
    inv[half:, half:] = low[...]
    inv[half:, :half] = -exact(low[...], exact(across, first_low[...], tn), nn)
    operands[2].wait()
    factor[:half, :half] = first_up[...] * (1.0 / root)
    factor[:half, half:] = across * (1.0 / root)
    factor[half:, half:] = up[...] * (1.0 / root)
    put = [pltpu.make_async_copy(factor, factor_out, sem.at[1])]
    put[0].start()

    mine = inv[pl.ds(pl.multiple_of(lax.axis_index("col") * width, width), width), :] * root
    high = mine.astype(bf16)
    rest = mine - high.astype(f32)
    left = jnp.concatenate([high, rest.astype(bf16)], axis=0)

    fetch.wait()
    every = lb // 4
    for k in range(lb):
        right = jnp.concatenate([whole[q, k] for q in range(parts)], axis=0)
        r = jnp.dot(left, right, preferred_element_type=f32)
        basis[:, k * bs:(k + 1) * bs] = r[:width] + r[width:]
        if k % every == every - 1:
            cut = pl.ds((k + 1 - every) * bs, every * bs)
            put.append(pltpu.make_async_copy(basis.at[:, cut], basis_out.at[:, cut],
                                             sem.at[2 + k // every]))
            put[-1].start()
    for copy in put:
        copy.wait()


def body(subspace, onsite, blocks, cols):
    row_count = lax.axis_size("row")
    part_width, local_rows = subspace.shape
    whole, gram, first_up, first_low = filtered(subspace, onsite, blocks, cols)
    full = gram.shape[0]
    half = full // 2
    root = math.sqrt(row_count * local_rows)
    vm = pltpu.VMEM
    return pl.pallas_call(
        functools.partial(finish_kernel, root),
        out_shape=(jax.ShapeDtypeStruct((part_width, local_rows), f32),
                   jax.ShapeDtypeStruct((full, full), f32)),
        in_specs=[pl.BlockSpec(memory_space=pltpu.HBM)] * 4,
        out_specs=[pl.BlockSpec(memory_space=pl.ANY)] * 2,
        scratch_shapes=[vm((part_width, local_rows), f32), vm((full, full), f32),
                        vm((half, half), f32), vm((half, half), f32), vm((full, full), f32),
                        vm((full, full), f32), vm((half, half), f32), vm((half, half), f32),
                        vm(whole.shape, bf16), pltpu.SemaphoreType.DMA((9,))],
        compiler_params=pltpu.CompilerParams(vmem_limit_bytes=60 * 1024 * 1024),
        name="finish",
    )(whole, gram, first_up, first_low)


def solution(mesh):
    in_specs = (P("col", "row"), P("row"), P(None, "row", None, None), P())
    out_specs = (P("col", "row"), P())
    return jax.shard_map(body, mesh=mesh, in_specs=in_specs, out_specs=out_specs, check_vma=False)
```
